32 devices in a mesh: groups: 2 (over x), seq: 16 (over z, y, core).
Axes of the slice: x: 2, y: 2, z: 4, core: 2. Of those that a mesh axis runs over, the one named last changes fastest.
Arguments:
- video_qkv: bfloat16 [4, 1536, 3, 4096], P('groups', 'seq'), parts along dimension 0, may hold values from -48 to 48
- video_cross_q: bfloat16 [4, 1536, 4096], P('groups', 'seq'), parts along dimension 0, may hold values from -48 to 48
- audio_kv_v: bfloat16 [4, 512, 2, 4096], P('groups', 'seq'), parts along dimension 0, may hold values from -4 to 4
- audio_qkv: bfloat16 [4, 512, 3, 2048], P('groups', 'seq'), parts along dimension 0, may hold values from -48 to 48
- audio_cross_q: bfloat16 [4, 512, 2048], P('groups', 'seq'), parts along dimension 0, may hold values from -48 to 48
- video_kv_a: bfloat16 [4, 1536, 2, 2048], P('groups', 'seq'), parts along dimension 0, may hold values from -4 to 4
- audio_valid: int32 [4], P('groups'), parts along dimension 0, may hold values from 256 to 512, as said below
- branch_prompt: int32 [4], P('groups'), parts along dimension 0, may hold values from 0 to 3
- video_gate: float32 [4, 4096], replicated, may hold values from 0.5 to 1.5
- audio_gate: float32 [4, 2048], replicated, may hold values from 0.5 to 1.5
Outputs:
- video_out: bfloat16 [4, 1536, 4096], P('groups', 'seq'), parts along dimension 0
- audio_out: bfloat16 [4, 512, 2048], P('groups', 'seq'), parts along dimension 0
The draws below stay inside these ranges and needn't reach their ends.
There are 2 independent parts, one for each index of `groups`. The reference program is written for one: setup_inputs(seed, part) draws one part's arguments, and reference() takes and returns one part's arrays. A program takes and returns all parts, laid end to end along the dimension named above; an argument that names none is the same for every part. Nothing has to cross between parts.
Inputs may be any that keep to these rules, and one draw needn't show every extreme that they name: `audio_valid`: at least one branch has all 512 audio tokens valid.
All inputs are finite; a program needn't handle non-finite values.
Results may differ from the reference program's by a relative error of at most 0.0058.
Values may be sent and summed in bfloat16 or wider, within the bound.
A program may use at most 128 MiB of HBM per device.

```python
import jax
import jax.numpy as jnp
from jax import lax

DV = 4096
HV = 32
DA = 2048
HA = 16
BR = 2
PROMPTS = 4
SV = 1536
SA = 512


def drawn_noise(key, marker, array_shape):
    return jnp.clip(jax.random.normal(jax.random.fold_in(key, marker), array_shape, jnp.float32), -4.0, 4.0)


def draw_video_qkv(key, part):
    noise = drawn_noise(key, 1, (BR, SV, 3, DV))
    return noise.astype(jnp.bfloat16)


def draw_video_cross_q(key, part):
    noise = drawn_noise(key, 2, (BR, SV, DV))
    return noise.astype(jnp.bfloat16)


def draw_audio_kv_v(key, part):
    noise = drawn_noise(key, 3, (BR, SA, 2, DV))
    return noise.astype(jnp.bfloat16)


def draw_audio_qkv(key, part):
    noise = drawn_noise(key, 4, (BR, SA, 3, DA))
    return noise.astype(jnp.bfloat16)


def draw_audio_cross_q(key, part):
    noise = drawn_noise(key, 5, (BR, SA, DA))
    return noise.astype(jnp.bfloat16)


def draw_video_kv_a(key, part):
    noise = drawn_noise(key, 6, (BR, SV, 2, DA))
    return noise.astype(jnp.bfloat16)


def draw_audio_valid(key, part):
    counts = jax.random.randint(jax.random.fold_in(key, 21), (BR,), SA // 2, SA + 1)
    full_branch = jax.random.randint(jax.random.fold_in(key, 22), (), 0, BR)
    return jnp.where(jnp.arange(BR) == full_branch, SA, counts).astype(jnp.int32)


def setup_inputs(seed: int = 0, part: int = 0) -> dict:
    arg_keys = jax.random.split(jax.random.key(seed), 11)
    part_keys = jax.random.split(jax.random.fold_in(arg_keys[10], part), 11)
    video_qkv = draw_video_qkv(jax.random.fold_in(jax.random.fold_in(arg_keys[10], part), 71), part)
    video_cross_q = draw_video_cross_q(jax.random.fold_in(jax.random.fold_in(arg_keys[10], part), 71), part)
    audio_kv_v = draw_audio_kv_v(jax.random.fold_in(jax.random.fold_in(arg_keys[10], part), 71), part)
    audio_qkv = draw_audio_qkv(jax.random.fold_in(jax.random.fold_in(arg_keys[10], part), 71), part)
    audio_cross_q = draw_audio_cross_q(jax.random.fold_in(jax.random.fold_in(arg_keys[10], part), 71), part)
    video_kv_a = draw_video_kv_a(jax.random.fold_in(jax.random.fold_in(arg_keys[10], part), 71), part)
    audio_valid = draw_audio_valid(jax.random.fold_in(jax.random.fold_in(arg_keys[10], part), 71), part)
    branch_prompt = jax.random.randint(part_keys[7], (BR,), 0, PROMPTS).astype(jnp.int32)
    video_gate = jnp.clip(jax.random.uniform(arg_keys[8], (PROMPTS, DV), jnp.float32, 0.5, 1.5), 0.5, 1.5)
    audio_gate = jnp.clip(jax.random.uniform(arg_keys[9], (PROMPTS, DA), jnp.float32, 0.5, 1.5), 0.5, 1.5)
    return {"video_qkv": video_qkv, "video_cross_q": video_cross_q, "audio_kv_v": audio_kv_v, "audio_qkv": audio_qkv, "audio_cross_q": audio_cross_q, "video_kv_a": video_kv_a, "audio_valid": audio_valid, "branch_prompt": branch_prompt, "video_gate": video_gate, "audio_gate": audio_gate}


def attend(queries, key_rows, value_rows, allowed):
    scores = jnp.dot(queries, key_rows.T, preferred_element_type=jnp.float32) * (queries.shape[-1] ** -0.5)
    if allowed is not None:
        scores = jnp.where(allowed[None, :], scores, -jnp.inf)
    row_max = jnp.max(scores, axis=1, keepdims=True)
    weights = jnp.exp(scores - row_max)
    shares = (weights / jnp.sum(weights, axis=1, keepdims=True)).astype(jnp.bfloat16)
    return jnp.dot(shares, value_rows, preferred_element_type=jnp.float32).astype(jnp.bfloat16)


def to_items(source, head_count):
    lead_count, row_count = source.shape[0], source.shape[1]
    middle = source.shape[2:-1]
    head_width = source.shape[-1] // head_count
    result = source.reshape((lead_count, row_count) + middle + (head_count, head_width))
    axes_order = (0, len(middle) + 2, 1) + tuple(range(2, len(middle) + 2)) + (len(middle) + 3,)
    result = jnp.transpose(result, axes_order)
    return result.reshape((lead_count * head_count, row_count) + middle + (head_width,))


def from_items(source, head_count):
    item_count, row_count, head_width = source.shape
    result = source.reshape(item_count // head_count, head_count, row_count, head_width)
    return jnp.transpose(result, (0, 2, 1, 3)).reshape(item_count // head_count, row_count, head_count * head_width)


def self_items(packed):
    return attend(packed[:, 0], packed[:, 1], packed[:, 2], None)


def self_masked(packed):
    return attend(packed[0][:, 0], packed[0][:, 1], packed[0][:, 2], packed[1])


def cross_masked(packed):
    return attend(packed[0], packed[1][:, 0], packed[1][:, 1], packed[2])


def cross_items(packed):
    return attend(packed[0], packed[1][:, 0], packed[1][:, 1], None)


def reference(video_qkv, video_cross_q, audio_kv_v, audio_qkv, audio_cross_q, video_kv_a, audio_valid, branch_prompt, video_gate, audio_gate):
    allowed = jnp.arange(SA, dtype=jnp.int32)[None, :] < audio_valid[:, None]
    video_self = lax.map(self_items, to_items(video_qkv, HV))
    video_cross = lax.map(cross_masked, (to_items(video_cross_q, HV), to_items(audio_kv_v, HV), jnp.repeat(allowed, HV, axis=0)))
    audio_self = lax.map(self_masked, (to_items(audio_qkv, HA), jnp.repeat(allowed, HA, axis=0)))
    audio_cross = lax.map(cross_items, (to_items(audio_cross_q, HA), to_items(video_kv_a, HA)))
    chosen = (branch_prompt[:, None] == jnp.arange(PROMPTS, dtype=jnp.int32)[None, :]).astype(jnp.float32)
    video_gates = jnp.dot(chosen, video_gate, precision=lax.Precision.HIGHEST)
    audio_gates = jnp.dot(chosen, audio_gate, precision=lax.Precision.HIGHEST)
    video_out = from_items(video_self, HV).astype(jnp.float32) + video_gates[:, None, :] * from_items(video_cross, HV).astype(jnp.float32)
    audio_out = from_items(audio_self, HA).astype(jnp.float32) + audio_gates[:, None, :] * from_items(audio_cross, HA).astype(jnp.float32)
    return video_out.astype(jnp.bfloat16), audio_out.astype(jnp.bfloat16)
```

```python
import functools

import jax
import jax.numpy as jnp
from jax import lax
from jax.experimental import pallas as pl
from jax.experimental.pallas import tpu as pltpu
from jax.sharding import PartitionSpec as P

HV = 32
HA = 16
HEAD = 128
PROMPTS = 4
MESH = pl.DeviceIdType.MESH


def attend(queries, key_rows, value_rows, bias):
    scores = lax.dot_general(
        queries, key_rows, (((1,), (1,)), ((), ())), preferred_element_type=jnp.float32
    ) * (HEAD**-0.5)
    if bias is not None:
        scores = scores + bias
    row_max = jnp.max(scores, axis=1, keepdims=True)
    weights = jnp.exp(scores - row_max)
    total = jnp.sum(weights, axis=1, keepdims=True)
    result = jnp.dot(
        weights.astype(jnp.bfloat16), value_rows, preferred_element_type=jnp.float32
    )
    return result / total, row_max + jnp.log(total)


def block_kernel(
    n,
    video_count,
    cross_count,
    audio_count,
    across_count,
    video_block,
    audio_block,
    video_qkv,
    video_q,
    audio_kv,
    audio_qkv,
    audio_q,
    video_kv,
    video_gate,
    audio_gate,
    audio_valid,
    branch_prompt,
    video_out,
    audio_out,
    video_qkv_in,
    video_q_in,
    audio_kv_in,
    both_q_in,
    own_kv_in,
    video_kv_in,
    video_res,
    cross_res,
    part_res,
    level_res,
    level_in,
    share_res,
    share_in,
    final_res,
    own_home,
    cross_home,
    video_sems,
    cross_sems,
    both_sems,
    kv_sems,
    pair_sems,
    send_sems,
    back_sems,
):
    me = lax.axis_index("seq")
    group = lax.axis_index("groups")
    video_local = video_out.shape[1]
    audio_local = audio_out.shape[1]

    barrier = pltpu.get_barrier_semaphore()

    def greet(k, carry):
        peer = lax.rem(me + k, n)
        pl.semaphore_signal(barrier, inc=1, device_id=(group, peer), device_id_type=MESH)
        return carry

    lax.fori_loop(1, n, greet, 0)
    pl.semaphore_wait(barrier, n - 1)

    video_rows = pl.ds(pl.multiple_of(me * video_local, video_local), video_local)
    audio_rows = pl.ds(pl.multiple_of(me * audio_local, audio_local), audio_local)

    near = n // 2
    half_first = (me // near) * near
    place_in_half = me - half_first
    half_rows = pl.ds(pl.multiple_of(place_in_half * video_local, video_local), video_local)

    def columns(head):
        return pl.ds(pl.multiple_of(head * HEAD, HEAD), HEAD)

    def video_parts(item, slot):
        branch, head = item // HV, lax.rem(item, HV)
        return (
            (
                video_qkv.at[branch, :, :, columns(head)],
                video_qkv_in.at[slot, :, video_rows],
                video_sems.at[slot],
            ),
        )

    def cross_q_parts(item, slot):
        branch, head = item // HV, lax.rem(item, HV)
        return (
            (
                video_q.at[branch, :, columns(head)],
                video_q_in.at[slot, half_rows],
                cross_sems.at[slot, 0],
            ),
        )

    def cross_kv_parts(item, slot):
        branch, head = item // HV, lax.rem(item, HV)
        return (
            (
                audio_kv.at[branch, :, :, columns(head)],
                audio_kv_in.at[slot, :, audio_rows],
                cross_sems.at[slot, 1],
            ),
        )

    half_audio_rows = pl.ds(pl.multiple_of(place_in_half * audio_local, audio_local), audio_local)

    def both_q_parts(item, slot):
        branch, head = item // HA, lax.rem(item, HA)
        return (
            (
                audio_qkv.at[branch, 0, :, columns(head)],
                both_q_in.at[slot, 0, audio_rows],
                both_sems.at[slot],
            ),
            (
                audio_q.at[branch, :, columns(head)],
                both_q_in.at[slot, 1, audio_rows],
                both_sems.at[slot],
            ),
        )

    def half_kv_parts(item, slot):
        branch, head = item // HA, lax.rem(item, HA)
        return (
            (
                audio_qkv.at[branch, 1:3, :, columns(head)],
                own_kv_in.at[slot, :, half_audio_rows],
                kv_sems.at[slot, 0],
            ),
            (
                video_kv.at[branch, :, :, columns(head)],
                video_kv_in.at[slot, :, half_rows],
                kv_sems.at[slot, 1],
            ),
        )

    def send(parts, count, slot, first_sem, first, span, ring):
        def items_of(peer):
            return parts(lax.rem(peer, ring) * count + slot, slot)

        def to_peer(k, carry):
            step = k // 2 + lax.rem(k, 2) * (span // 2)
            peer = first + lax.rem(me - first + step, span)
            for place, (source, target, sem) in enumerate(items_of(peer)):
                pltpu.make_async_remote_copy(
                    src_ref=source,
                    dst_ref=target,
                    send_sem=send_sems.at[first_sem + (0 if first_sem == 3 else place)],
                    recv_sem=sem,
                    device_id=(group, peer),
                    device_id_type=MESH,
                ).start()
            return carry

        lax.fori_loop(1, span, to_peer, 0)
        for source, target, sem in items_of(me):
            pltpu.make_async_copy(source, target, sem).start()

    per_video = cross_count // (video_count - audio_count)
    per_audio = across_count // audio_count

    def send_video(slot, carry):
        send(video_parts, video_count, slot, 0, 0, n, n)
        return carry

    def send_crosses(slot, carry):
        first = (slot - audio_count) * per_video

        def send_cross(j, inner):
            send(cross_kv_parts, cross_count, first + j, 2, 0, n, near)
            send(cross_q_parts, cross_count, first + j, 1, half_first, near, near)
            return inner

        lax.fori_loop(0, per_video, send_cross, 0)
        return carry

    def send_audio(slot, carry):
        def send_one(j, inner):
            item_slot = slot * per_audio + j
            send(both_q_parts, across_count, item_slot, 3, 0, n, near)
            send(half_kv_parts, across_count, item_slot, 4, half_first, near, near)
            return inner

        lax.fori_loop(0, per_audio, send_one, 0)
        return carry

    def early(slot, carry, video, other):
        video(slot, carry)
        return other(slot, carry)

    lax.fori_loop(
        0, audio_count, functools.partial(early, video=send_video, other=send_audio), 0
    )
    lax.fori_loop(
        audio_count,
        video_count,
        functools.partial(early, video=send_video, other=send_crosses),
        0,
    )

    def mask(branch):
        positions = lax.broadcasted_iota(jnp.int32, (1, audio_kv_in.shape[2]), 1)
        return jnp.where(positions < audio_valid[branch], 0.0, -jnp.inf)

    def gate_of(gates, branch, here):
        return sum(
            (branch_prompt[branch] == p).astype(jnp.int32).astype(jnp.float32)
            * gates[p : p + 1, here]
            for p in range(PROMPTS)
        )

    def settle(ref, sem):
        pltpu.make_async_copy(ref, ref, sem).wait()

    def give_back(result, slot, out, branch, head, local, base, first, count, place):
        def to_peer(j, carry):
            peer = base + first + j
            source = result.at[slot, pl.ds(pl.multiple_of((first + j) * local, local), local)]
            target = out.at[branch, :, columns(head)]

            @pl.when(peer == me)
            def _():
                pltpu.make_async_copy(source, target, back_sems.at[place]).start()

            @pl.when(peer != me)
            def _():
                pltpu.make_async_remote_copy(
                    src_ref=source,
                    dst_ref=target,
                    send_sem=send_sems.at[6 + place],
                    recv_sem=back_sems.at[place],
                    device_id=(group, peer),
                    device_id_type=MESH,
                ).start()

            return carry

        lax.fori_loop(0, count, to_peer, 0)

    def video_item(slot, carry):
        item = me * video_count + slot
        branch, head = item // HV, lax.rem(item, HV)
        settle(video_qkv_in.at[slot], video_sems.at[slot])
        block = video_block * video_local

        def rows(i, inner):
            here = pl.ds(pl.multiple_of(i * block, block), block)
            own, _ = attend(
                video_qkv_in[slot, 0, here], video_qkv_in[slot, 1], video_qkv_in[slot, 2], None
            )
            video_res[slot, here] = own.astype(jnp.bfloat16)
            give_back(
                video_res, slot, own_home, branch, head, video_local, 0, i * video_block,
                video_block, 0,
            )
            return inner

        lax.fori_loop(0, n // video_block, rows, 0)
        return carry

    def cross_items(slot, carry):
        def cross(j, inner):
            cross_item((slot - audio_count) * per_video + j)
            return inner

        lax.fori_loop(0, per_video, cross, 0)
        return carry

    def cross_item(slot):
        item = place_in_half * cross_count + slot
        branch, head = item // HV, lax.rem(item, HV)
        settle(video_q_in.at[slot], cross_sems.at[slot, 0])
        settle(audio_kv_in.at[slot], cross_sems.at[slot, 1])
        block = video_block * video_local

        def rows(i, inner):
            here = pl.ds(pl.multiple_of(i * block, block), block)
            cross, _ = attend(
                video_q_in[slot, here], audio_kv_in[slot, 0], audio_kv_in[slot, 1], mask(branch)
            )
            cross_res[slot, here] = cross.astype(jnp.bfloat16)
            give_back(
                cross_res, slot, cross_home, branch, head, video_local, half_first,
                i * video_block, video_block, 2,
            )
            return inner

        lax.fori_loop(0, near // video_block, rows, 0)

    my_half = me // near
    partner = lax.rem(me + near, n)
    half_audio = near * audio_local
    chunks = n * audio_local // HEAD
    half_chunks = chunks // 2

    def half_mask(branch):
        positions = lax.broadcasted_iota(jnp.int32, (1, half_audio), 1) + my_half * half_audio
        return jnp.where(positions < audio_valid[branch], 0.0, -1e30)

    def audio_place(slot):
        item = place_in_half * across_count + slot
        return item // HA, lax.rem(item, HA)

    def to_partner(source, target, place, slot):
        pltpu.make_async_remote_copy(
            src_ref=source.at[slot],
            dst_ref=target.at[slot],
            send_sem=send_sems.at[9 + place],
            recv_sem=pair_sems.at[place, slot],
            device_id=(group, partner),
            device_id_type=MESH,
        ).start()

    def audio_item(slot):
        branch, head = audio_place(slot)
        settle(both_q_in.at[slot], both_sems.at[slot])
        settle(own_kv_in.at[slot], kv_sems.at[slot, 0])
        settle(video_kv_in.at[slot], kv_sems.at[slot, 1])
        block = audio_block * audio_local
        per_block = block // HEAD

        def rows(i, inner):
            here = pl.ds(pl.multiple_of(i * block, block), block)
            for kind, (keys, bias) in enumerate(
                ((own_kv_in, half_mask(branch)), (video_kv_in, None))
            ):
                part, level = attend(
                    both_q_in[slot, kind, here], keys[slot, 0], keys[slot, 1], bias
                )
                part_res[slot, kind, here] = part
                for c in range(per_block):
                    column = jnp.broadcast_to(level[c * HEAD : (c + 1) * HEAD], (HEAD, HEAD))
                    level_res[slot, kind * chunks + i * per_block + c] = jnp.transpose(column)[0:1]
            return inner

        lax.fori_loop(0, n // audio_block, rows, 0)
        to_partner(level_res, level_in, 0, slot)

    def audio_items(slot, carry):
        def one(j, inner):
            audio_item(slot * per_audio + j)
            return inner

        lax.fori_loop(0, per_audio, one, 0)
        return carry

    def weighted(slot, chunk, gate):
        here = pl.ds(pl.multiple_of(chunk * HEAD, HEAD), HEAD)
        terms = []
        for kind in range(2):
            gap = level_in[slot, kind * chunks + chunk] - level_res[slot, kind * chunks + chunk]
            weight = jnp.transpose(jnp.broadcast_to(1.0 / (1.0 + jnp.exp(gap)), (HEAD, HEAD)))
            terms.append(weight * part_res[slot, kind, here])
        return terms[0] + gate * terms[1]

    def audio_share(slot, carry):
        branch, head = audio_place(slot)
        settle(level_in.at[slot], pair_sems.at[0, slot])
        gate = gate_of(audio_gate, branch, columns(head))
        for c in range(half_chunks):
            share_res[slot, c * HEAD : (c + 1) * HEAD] = weighted(
                slot, (1 - my_half) * half_chunks + c, gate
            ).astype(jnp.bfloat16)
        to_partner(share_res, share_in, 1, slot)
        return carry

    def audio_final(slot, carry):
        branch, head = audio_place(slot)
        settle(share_in.at[slot], pair_sems.at[1, slot])
        gate = gate_of(audio_gate, branch, columns(head))
        for c in range(half_chunks):
            here = slice(c * HEAD, (c + 1) * HEAD)
            final_res[slot, here] = (
                weighted(slot, my_half * half_chunks + c, gate)
                + share_in[slot, here].astype(jnp.float32)
            ).astype(jnp.bfloat16)
        give_back(
            final_res, slot, audio_out, branch, head, audio_local, half_first, 0, near, 1
        )
        return carry

    def late(slot, carry):
        video_item(slot, carry)

        @pl.when(slot == audio_count)
        def _():
            lax.fori_loop(0, across_count, audio_share, 0)

        return cross_items(slot, carry)

    lax.fori_loop(
        0, audio_count, functools.partial(early, video=video_item, other=audio_items), 0
    )
    lax.fori_loop(audio_count, video_count, late, 0)
    lax.fori_loop(0, across_count, audio_final, 0)

    settle(own_home, back_sems.at[0])
    settle(cross_home, back_sems.at[2])
    width = 512

    def combine(i, carry):
        here = pl.ds(pl.multiple_of(i * width, width), width)
        for branch in range(own_home.shape[0]):
            video_out[branch, :, here] = (
                own_home[branch, :, here].astype(jnp.float32)
                + gate_of(video_gate, branch, here) * cross_home[branch, :, here].astype(jnp.float32)
            ).astype(jnp.bfloat16)
        return carry

    lax.fori_loop(0, video_out.shape[2] // width, combine, 0)

    settle(audio_out, back_sems.at[1])

    far_video = pl.ds(0, (n - 1) * video_local)
    far_audio = pl.ds(0, (n - 1) * audio_local)
    far_half = pl.ds(0, (near - 1) * video_local)
    settle(video_qkv_in.at[:, :, far_video], send_sems.at[0])
    settle(video_q_in.at[:, far_half], send_sems.at[1])
    settle(audio_kv_in.at[:, :, far_audio], send_sems.at[2])
    settle(both_q_in.at[:, :, far_audio], send_sems.at[3])
    settle(own_kv_in.at[:, :, pl.ds(0, (near - 1) * audio_local)], send_sems.at[4])
    settle(video_kv_in.at[:, :, far_half], send_sems.at[5])
    settle(video_res.at[:, far_video], send_sems.at[6])
    settle(final_res.at[:, pl.ds(0, (near - 1) * audio_local)], send_sems.at[7])
    settle(cross_res.at[:, far_half], send_sems.at[8])
    settle(level_res, send_sems.at[9])
    settle(share_res, send_sems.at[10])


def kinds_first(source):
    return jnp.transpose(source, (0, 2, 1, 3))


def on_device(
    n,
    video_qkv,
    video_cross_q,
    audio_kv_v,
    audio_qkv,
    audio_cross_q,
    video_kv_a,
    audio_valid,
    branch_prompt,
    video_gate,
    audio_gate,
):
    branches, video_local = video_cross_q.shape[:2]
    audio_local = audio_cross_q.shape[1]
    video_all, audio_all = video_local * n, audio_local * n
    video_count, audio_count = branches * HV // n, branches * HA // n
    near = n // 2
    cross_count, across_count = branches * HV // near, branches * HA // near
    hbm = pl.BlockSpec(memory_space=pl.ANY)
    vmem = pl.BlockSpec(memory_space=pltpu.VMEM)
    smem = pl.BlockSpec(memory_space=pltpu.SMEM)
    half = jnp.bfloat16
    return tuple(
        pl.pallas_call(
            functools.partial(
                block_kernel, n, video_count, cross_count, audio_count, across_count, min(4, near), min(8, n)
            ),
            out_shape=(
                jax.ShapeDtypeStruct(video_cross_q.shape, half),
                jax.ShapeDtypeStruct(audio_cross_q.shape, half),
            ),
            in_specs=[hbm] * 6 + [vmem] * 2 + [smem] * 2,
            out_specs=(vmem, vmem),
            scratch_shapes=[
                pltpu.VMEM((video_count, 3, video_all, HEAD), half),
                pltpu.VMEM((cross_count, near * video_local, HEAD), half),
                pltpu.VMEM((cross_count, 2, audio_all, HEAD), half),
                pltpu.VMEM((across_count, 2, audio_all, HEAD), half),
                pltpu.VMEM((across_count, 2, near * audio_local, HEAD), half),
                pltpu.VMEM((across_count, 2, near * video_local, HEAD), half),
                pltpu.VMEM((video_count, video_all, HEAD), half),
                pltpu.VMEM((cross_count, near * video_local, HEAD), half),
                pltpu.VMEM((across_count, 2, audio_all, HEAD), jnp.float32),
                pltpu.VMEM((across_count, 2 * audio_all // HEAD, 1, HEAD), jnp.float32),
                pltpu.VMEM((across_count, 2 * audio_all // HEAD, 1, HEAD), jnp.float32),
                pltpu.VMEM((across_count, near * audio_local, HEAD), half),
                pltpu.VMEM((across_count, near * audio_local, HEAD), half),
                pltpu.VMEM((across_count, near * audio_local, HEAD), half),
                pltpu.VMEM(video_cross_q.shape, half),
                pltpu.VMEM(video_cross_q.shape, half),
                pltpu.SemaphoreType.DMA((video_count,)),
                pltpu.SemaphoreType.DMA((cross_count, 2)),
                pltpu.SemaphoreType.DMA((across_count,)),
                pltpu.SemaphoreType.DMA((across_count, 2)),
                pltpu.SemaphoreType.DMA((2, across_count)),
                pltpu.SemaphoreType.DMA((11,)),
                pltpu.SemaphoreType.DMA((3,)),
            ],
            compiler_params=pltpu.CompilerParams(
                collective_id=0, has_side_effects=True, vmem_limit_bytes=52 * 2**20
            ),
        )(
            kinds_first(video_qkv),
            video_cross_q,
            kinds_first(audio_kv_v),
            kinds_first(audio_qkv),
            audio_cross_q,
            kinds_first(video_kv_a),
            video_gate,
            audio_gate,
            audio_valid,
            branch_prompt,
        )
    )


def solution(mesh):
    placed = (
        P("groups", "seq", None, None),
        P("groups", "seq", None),
        P("groups", "seq", None, None),
        P("groups", "seq", None, None),
        P("groups", "seq", None),
        P("groups", "seq", None, None),
        P("groups"),
        P("groups"),
        P(),
        P(),
    )
    return jax.shard_map(
        functools.partial(on_device, mesh.shape["seq"]),
        mesh=mesh,
        in_specs=placed,
        out_specs=(P("groups", "seq", None), P("groups", "seq", None)),
        check_vma=False,
    )
```

```python
import functools

import jax
import jax.numpy as jnp
from jax import lax
from jax.experimental import pallas as pl
from jax.experimental.pallas import tpu as pltpu
from jax.sharding import PartitionSpec as P

HV = 32
HA = 16
HEAD = 128
PROMPTS = 4
MESH = pl.DeviceIdType.MESH
AHEAD = 2


def attend(queries, key_rows, value_rows, bias):
    scores = lax.dot_general(
        queries, key_rows, (((1,), (1,)), ((), ())), preferred_element_type=jnp.float32
    ) * (HEAD**-0.5)
    if bias is not None:
        scores = scores + bias
    row_max = jnp.max(scores, axis=1, keepdims=True)
    weights = jnp.exp(scores - row_max)
    total = jnp.sum(weights, axis=1, keepdims=True)
    result = jnp.dot(
        weights.astype(jnp.bfloat16), value_rows, preferred_element_type=jnp.float32
    )
    return result / total, row_max + jnp.log(total)


def block_kernel(
    n,
    video_outer,
    video_inner,
    cross_count,
    audio_outer,
    audio_inner,
    video_block,
    audio_block,
    video_qkv,
    video_q,
    audio_kv,
    audio_qkv,
    audio_q,
    video_kv,
    video_gate,
    audio_gate,
    audio_valid,
    branch_prompt,
    video_out,
    audio_out,
    video_qkv_in,
    video_q_in,
    audio_kv_in,
    both_q_in,
    own_kv_in,
    video_kv_in,
    video_res,
    cross_res,
    part_res,
    level_res,
    level_in,
    share_res,
    share_in,
    final_res,
    own_home,
    cross_home,
    video_sems,
    cross_sems,
    both_sems,
    kv_sems,
    pair_sems,
    send_sems,
    back_sems,
):
    me = lax.axis_index("seq")
    group = lax.axis_index("groups")
    video_local = video_out.shape[1]
    audio_local = audio_out.shape[1]

    barrier = pltpu.get_barrier_semaphore()

    def greet(k, carry):
        peer = lax.rem(me + k, n)
        pl.semaphore_signal(barrier, inc=1, device_id=(group, peer), device_id_type=MESH)
        return carry

    lax.fori_loop(1, n, greet, 0)
    pl.semaphore_wait(barrier, n - 1)

    video_rows = pl.ds(pl.multiple_of(me * video_local, video_local), video_local)
    audio_rows = pl.ds(pl.multiple_of(me * audio_local, audio_local), audio_local)

    near, quarter = n // 2, n // 4
    my_half = me // near
    half_first = my_half * near
    place_in_half = me - half_first
    half_rows = pl.ds(pl.multiple_of(place_in_half * video_local, video_local), video_local)
    half_audio_rows = pl.ds(pl.multiple_of(place_in_half * audio_local, audio_local), audio_local)

    def is_inner(device):
        q = device // quarter
        return (q * (3 - q)) // 2

    inner = is_inner(me)
    outer_in_half = my_half * 3 * quarter

    def columns(head):
        return pl.ds(pl.multiple_of(head * HEAD, HEAD), HEAD)

    def video_place(device, slot):
        here = is_inner(device)
        high = device // near
        outside = (device - high * 2 * quarter) * video_outer + slot
        inside = 2 * quarter * video_outer + (device - quarter) * video_inner + slot
        item = outside + here * (inside - outside)
        return item // HV, lax.rem(item, HV)

    def cross_place(device, slot):
        item = lax.rem(device, near) * cross_count + slot
        return item // HV, lax.rem(item, HV)

    def audio_place(device, slot):
        here = is_inner(device)
        r = lax.rem(device, quarter)
        outside = r * audio_outer + slot
        inside = quarter * audio_outer + r * audio_inner + slot
        item = outside + here * (inside - outside)
        return item // HA, lax.rem(item, HA)

    def video_parts(peer, slot):
        branch, head = video_place(peer, slot)
        return (
            (
                video_qkv.at[branch, :, :, columns(head)],
                video_qkv_in.at[slot, :, video_rows],
                video_sems.at[slot],
            ),
        )

    def cross_q_parts(peer, slot):
        branch, head = cross_place(peer, slot)
        return (
            (
                video_q.at[branch, :, columns(head)],
                video_q_in.at[slot, half_rows],
                cross_sems.at[slot, 0],
            ),
        )

    def cross_kv_parts(peer, slot):
        branch, head = cross_place(peer, slot)
        return (
            (
                audio_kv.at[branch, :, :, columns(head)],
                audio_kv_in.at[slot, :, audio_rows],
                cross_sems.at[slot, 1],
            ),
        )

    def both_q_parts(peer, slot):
        branch, head = audio_place(peer, slot)
        return (
            (
                audio_qkv.at[branch, 0, :, columns(head)],
                both_q_in.at[slot, 0, audio_rows],
                both_sems.at[slot],
            ),
            (
                audio_q.at[branch, :, columns(head)],
                both_q_in.at[slot, 1, audio_rows],
                both_sems.at[slot],
            ),
        )

    def own_kv_parts(peer, slot):
        branch, head = audio_place(peer, slot)
        return (
            (
                audio_qkv.at[branch, 1:3, :, columns(head)],
                own_kv_in.at[slot, :, half_audio_rows],
                kv_sems.at[slot, 0],
            ),
        )

    def video_kv_parts(peer, slot):
        branch, head = audio_place(peer, slot)
        return (
            (
                video_kv.at[branch, :, :, columns(head)],
                video_kv_in.at[slot, :, half_rows],
                kv_sems.at[slot, 1],
            ),
        )

    def send(parts, slot, send_sem, first, span):
        place = lax.rem(me - first + n, n)
        member = 1 - jnp.minimum(place // span, 1)

        def to_peer(k, carry):
            step = k // 2 + lax.rem(k, 2) * (span // 2)
            peer = lax.rem(first + lax.rem(place + step, span), n)
            for source, target, sem in parts(peer, slot):
                pltpu.make_async_remote_copy(
                    src_ref=source,
                    dst_ref=target,
                    send_sem=send_sems.at[send_sem],
                    recv_sem=sem,
                    device_id=(group, peer),
                    device_id_type=MESH,
                ).start()
            return carry

        lax.fori_loop(member, span, to_peer, 0)

        @pl.when(member == 1)
        def _():
            for source, target, sem in parts(me, slot):
                pltpu.make_async_copy(source, target, sem).start()

    steps = video_inner + 1

    def cross_before(step):
        return (jnp.maximum(step, 1) - 1) * cross_count // (steps - 1)

    def send_step(step, carry):
        def send_cross(slot, inner_carry):
            send(cross_kv_parts, slot, 3, 0, n)
            send(cross_q_parts, slot, 2, half_first, near)
            return inner_carry

        lax.fori_loop(cross_before(step), cross_before(step + 1), send_cross, 0)
        @pl.when(step < video_outer)
        def _():
            send(video_parts, step, 0, 0, n)

        @pl.when((step >= video_outer) & (step < video_inner))
        def _():
            send(video_parts, step, 1, quarter, 2 * quarter)

        @pl.when(step < audio_inner)
        def _():
            send(both_q_parts, step, 4, 0, n)
            send(own_kv_parts, step, 6, half_first, near)
            send(video_kv_parts, step, 7, half_first, near)

        @pl.when((step >= audio_inner) & (step < audio_outer))
        def _():
            send(both_q_parts, step, 5, 3 * quarter, 2 * quarter)
            send(own_kv_parts, step, 8, outer_in_half, quarter)
            send(video_kv_parts, step, 9, outer_in_half, quarter)


        return carry

    lax.fori_loop(0, min(AHEAD, steps), send_step, 0)

    def mask(branch):
        positions = lax.broadcasted_iota(jnp.int32, (1, audio_kv_in.shape[2]), 1)
        return jnp.where(positions < audio_valid[branch], 0.0, -jnp.inf)

    def gate_of(gates, branch, here):
        return sum(
            (branch_prompt[branch] == p).astype(jnp.int32).astype(jnp.float32)
            * gates[p : p + 1, here]
            for p in range(PROMPTS)
        )

    def settle(ref, sem):
        pltpu.make_async_copy(ref, ref, sem).wait()

    def give_back(result, slot, out, branch, head, local, base, first, count, place):
        def to_peer(j, carry):
            peer = base + first + j
            source = result.at[slot, pl.ds(pl.multiple_of((first + j) * local, local), local)]
            target = out.at[branch, :, columns(head)]

            @pl.when(peer == me)
            def _():
                pltpu.make_async_copy(source, target, back_sems.at[place]).start()

            @pl.when(peer != me)
            def _():
                pltpu.make_async_remote_copy(
                    src_ref=source,
                    dst_ref=target,
                    send_sem=send_sems.at[10 + place],
                    recv_sem=back_sems.at[place],
                    device_id=(group, peer),
                    device_id_type=MESH,
                ).start()

            return carry

        lax.fori_loop(0, count, to_peer, 0)

    def video_item(slot):
        branch, head = video_place(me, slot)
        settle(video_qkv_in.at[slot], video_sems.at[slot])
        block = video_block * video_local

        def rows(i, inner):
            here = pl.ds(pl.multiple_of(i * block, block), block)
            own, _ = attend(
                video_qkv_in[slot, 0, here], video_qkv_in[slot, 1], video_qkv_in[slot, 2], None
            )
            video_res[slot, here] = own.astype(jnp.bfloat16)
            give_back(
                video_res, slot, own_home, branch, head, video_local, 0, i * video_block,
                video_block, 0,
            )
            return inner

        lax.fori_loop(0, n // video_block, rows, 0)

    def cross_item(slot, carry):
        branch, head = cross_place(me, slot)
        settle(video_q_in.at[slot], cross_sems.at[slot, 0])
        settle(audio_kv_in.at[slot], cross_sems.at[slot, 1])
        block = video_block * video_local

        def rows(i, inner):
            here = pl.ds(pl.multiple_of(i * block, block), block)
            cross, _ = attend(
                video_q_in[slot, here], audio_kv_in[slot, 0], audio_kv_in[slot, 1], mask(branch)
            )
            cross_res[slot, here] = cross.astype(jnp.bfloat16)
            give_back(
                cross_res, slot, cross_home, branch, head, video_local, half_first,
                i * video_block, video_block, 2,
            )
            return inner

        lax.fori_loop(0, near // video_block, rows, 0)
        return carry

    partner = (3 - me // quarter) * quarter + lax.rem(me, quarter)
    half_audio = near * audio_local
    chunks = n * audio_local // HEAD
    half_chunks = chunks // 2

    def half_mask(branch):
        positions = lax.broadcasted_iota(jnp.int32, (1, half_audio), 1) + my_half * half_audio
        return jnp.where(positions < audio_valid[branch], 0.0, -1e30)

    def to_partner(source, target, place, slot):
        pltpu.make_async_remote_copy(
            src_ref=source.at[slot],
            dst_ref=target.at[slot],
            send_sem=send_sems.at[13 + place],
            recv_sem=pair_sems.at[place, slot],
            device_id=(group, partner),
            device_id_type=MESH,
        ).start()

    def audio_item(slot):
        branch, head = audio_place(me, slot)
        settle(both_q_in.at[slot], both_sems.at[slot])
        settle(own_kv_in.at[slot], kv_sems.at[slot, 0])
        settle(video_kv_in.at[slot], kv_sems.at[slot, 1])
        block = audio_block * audio_local
        per_block = block // HEAD

        def rows(i, inner):
            here = pl.ds(pl.multiple_of(i * block, block), block)
            for kind, (keys, bias) in enumerate(
                ((own_kv_in, half_mask(branch)), (video_kv_in, None))
            ):
                part, level = attend(
                    both_q_in[slot, kind, here], keys[slot, 0], keys[slot, 1], bias
                )
                part_res[slot, kind, here] = part
                for c in range(per_block):
                    column = jnp.broadcast_to(level[c * HEAD : (c + 1) * HEAD], (HEAD, HEAD))
                    level_res[slot, kind * chunks + i * per_block + c] = jnp.transpose(column)[0:1]
            return inner

        lax.fori_loop(0, n // audio_block, rows, 0)
        to_partner(level_res, level_in, 0, slot)

    def weighted(slot, chunk, gate):
        here = pl.ds(pl.multiple_of(chunk * HEAD, HEAD), HEAD)
        terms = []
        for kind in range(2):
            gap = level_in[slot, kind * chunks + chunk] - level_res[slot, kind * chunks + chunk]
            weight = jnp.transpose(jnp.broadcast_to(1.0 / (1.0 + jnp.exp(gap)), (HEAD, HEAD)))
            terms.append(weight * part_res[slot, kind, here])
        return terms[0] + gate * terms[1]

    def audio_share(slot):
        branch, head = audio_place(me, slot)
        settle(level_in.at[slot], pair_sems.at[0, slot])
        gate = gate_of(audio_gate, branch, columns(head))
        for c in range(half_chunks):
            share_res[slot, c * HEAD : (c + 1) * HEAD] = weighted(
                slot, (1 - my_half) * half_chunks + c, gate
            ).astype(jnp.bfloat16)
        to_partner(share_res, share_in, 1, slot)

    def audio_final(slot):
        branch, head = audio_place(me, slot)
        settle(share_in.at[slot], pair_sems.at[1, slot])
        gate = gate_of(audio_gate, branch, columns(head))
        for c in range(half_chunks):
            here = slice(c * HEAD, (c + 1) * HEAD)
            final_res[slot, here] = (
                weighted(slot, my_half * half_chunks + c, gate)
                + share_in[slot, here].astype(jnp.float32)
            ).astype(jnp.bfloat16)
        give_back(
            final_res, slot, audio_out, branch, head, audio_local, half_first, 0, near, 1
        )

    my_video = video_outer + inner * (video_inner - video_outer)
    my_audio = audio_outer + inner * (audio_inner - audio_outer)

    def work_step(step, carry):
        @pl.when(step + AHEAD < steps)
        def _():
            send_step(step + AHEAD, 0)

        @pl.when(step < my_audio)
        def _():
            audio_item(step)

        @pl.when(step < my_video)
        def _():
            video_item(step)

        @pl.when((step >= 1) & (step - 1 < my_audio))
        def _():
            audio_share(step - 1)

        lax.fori_loop(cross_before(step), cross_before(step + 1), cross_item, 0)

        @pl.when((step >= 2) & (step - 2 < my_audio))
        def _():
            audio_final(step - 2)

        return carry

    lax.fori_loop(0, steps, work_step, 0)

    @pl.when(my_audio == steps - 1)
    def _():
        audio_final(steps - 2)

    settle(own_home, back_sems.at[0])
    settle(cross_home, back_sems.at[2])
    width = 512

    def combine(i, carry):
        here = pl.ds(pl.multiple_of(i * width, width), width)
        for branch in range(own_home.shape[0]):
            video_out[branch, :, here] = (
                own_home[branch, :, here].astype(jnp.float32)
                + gate_of(video_gate, branch, here) * cross_home[branch, :, here].astype(jnp.float32)
            ).astype(jnp.bfloat16)
        return carry

    lax.fori_loop(0, video_out.shape[2] // width, combine, 0)

    settle(audio_out, back_sems.at[1])

    far_half = pl.ds(0, (near - 1) * video_local)
    far_video = pl.ds(0, (n - 1) * video_local)

    def few(count, local):
        return pl.ds(0, count * local)

    settle(video_qkv_in.at[0:video_outer, :, far_video], send_sems.at[0])
    settle(video_q_in.at[:, far_half], send_sems.at[2])
    settle(audio_kv_in.at[:, :, few(n - 1, audio_local)], send_sems.at[3])
    settle(both_q_in.at[0:audio_inner, :, few(n - 1, audio_local)], send_sems.at[4])
    settle(own_kv_in.at[0:audio_inner, :, few(near - 1, audio_local)], send_sems.at[6])
    settle(video_kv_in.at[0:audio_inner, :, far_half], send_sems.at[7])
    settle(cross_res.at[:, far_half], send_sems.at[12])

    for here in range(2):

        @pl.when(inner == here)
        def _():
            away = 1 - here
            more_video = pl.ds(video_outer, video_inner - video_outer)
            more_audio = pl.ds(audio_inner, audio_outer - audio_inner)
            videos = pl.ds(0, (video_outer, video_inner)[here])
            audios = pl.ds(0, (audio_outer, audio_inner)[here])
            settle(video_qkv_in.at[more_video, :, few(2 * quarter - here, video_local)], send_sems.at[1])
            settle(both_q_in.at[more_audio, :, few(2 * quarter - away, audio_local)], send_sems.at[5])
            settle(own_kv_in.at[more_audio, :, few(quarter - away, audio_local)], send_sems.at[8])
            settle(video_kv_in.at[more_audio, :, few(quarter - away, video_local)], send_sems.at[9])
            settle(video_res.at[videos, far_video], send_sems.at[10])
            settle(final_res.at[audios, few(near - 1, audio_local)], send_sems.at[11])
            settle(level_res.at[audios], send_sems.at[13])
            settle(share_res.at[audios], send_sems.at[14])


def kinds_first(source):
    return jnp.transpose(source, (0, 2, 1, 3))


def shares(total):
    return total // 4, total - total // 4


def on_device(
    n,
    video_qkv,
    video_cross_q,
    audio_kv_v,
    audio_qkv,
    audio_cross_q,
    video_kv_a,
    audio_valid,
    branch_prompt,
    video_gate,
    audio_gate,
):
    branches, video_local = video_cross_q.shape[:2]
    audio_local = audio_cross_q.shape[1]
    video_all, audio_all = video_local * n, audio_local * n
    near, quarter = n // 2, n // 4
    video_outer, video_inner = 2, 6
    cross_count = branches * HV // near
    audio_inner, audio_outer = 2, 6
    hbm = pl.BlockSpec(memory_space=pl.ANY)
    vmem = pl.BlockSpec(memory_space=pltpu.VMEM)
    smem = pl.BlockSpec(memory_space=pltpu.SMEM)
    half = jnp.bfloat16
    return tuple(
        pl.pallas_call(
            functools.partial(
                block_kernel,
                n,
                video_outer,
                video_inner,
                cross_count,
                audio_outer,
                audio_inner,
                min(4, near),
                min(8, n),
            ),
            out_shape=(
                jax.ShapeDtypeStruct(video_cross_q.shape, half),
                jax.ShapeDtypeStruct(audio_cross_q.shape, half),
            ),
            in_specs=[hbm] * 6 + [vmem] * 2 + [smem] * 2,
            out_specs=(vmem, vmem),
            scratch_shapes=[
                pltpu.VMEM((video_inner, 3, video_all, HEAD), half),
                pltpu.VMEM((cross_count, near * video_local, HEAD), half),
                pltpu.VMEM((cross_count, 2, audio_all, HEAD), half),
                pltpu.VMEM((audio_outer, 2, audio_all, HEAD), half),
                pltpu.VMEM((audio_outer, 2, near * audio_local, HEAD), half),
                pltpu.VMEM((audio_outer, 2, near * video_local, HEAD), half),
                pltpu.VMEM((video_inner, video_all, HEAD), half),
                pltpu.VMEM((cross_count, near * video_local, HEAD), half),
                pltpu.VMEM((audio_outer, 2, audio_all, HEAD), jnp.float32),
                pltpu.VMEM((audio_outer, 2 * audio_all // HEAD, 1, HEAD), jnp.float32),
                pltpu.VMEM((audio_outer, 2 * audio_all // HEAD, 1, HEAD), jnp.float32),
                pltpu.VMEM((audio_outer, near * audio_local, HEAD), half),
                pltpu.VMEM((audio_outer, near * audio_local, HEAD), half),
                pltpu.VMEM((audio_outer, near * audio_local, HEAD), half),
                pltpu.VMEM(video_cross_q.shape, half),
                pltpu.VMEM(video_cross_q.shape, half),
                pltpu.SemaphoreType.DMA((video_inner,)),
                pltpu.SemaphoreType.DMA((cross_count, 2)),
                pltpu.SemaphoreType.DMA((audio_outer,)),
                pltpu.SemaphoreType.DMA((audio_outer, 2)),
                pltpu.SemaphoreType.DMA((2, audio_outer)),
                pltpu.SemaphoreType.DMA((15,)),
                pltpu.SemaphoreType.DMA((3,)),
            ],
            compiler_params=pltpu.CompilerParams(
                collective_id=0, has_side_effects=True, vmem_limit_bytes=52 * 2**20
            ),
        )(
            kinds_first(video_qkv),
            video_cross_q,
            kinds_first(audio_kv_v),
            kinds_first(audio_qkv),
            audio_cross_q,
            kinds_first(video_kv_a),
            video_gate,
            audio_gate,
            audio_valid,
            branch_prompt,
        )
    )


def solution(mesh):
    placed = (
        P("groups", "seq", None, None),
        P("groups", "seq", None),
        P("groups", "seq", None, None),
        P("groups", "seq", None, None),
        P("groups", "seq", None),
        P("groups", "seq", None, None),
        P("groups"),
        P("groups"),
        P(),
        P(),
    )
    return jax.shard_map(
        functools.partial(on_device, mesh.shape["seq"]),
        mesh=mesh,
        in_specs=placed,
        out_specs=(P("groups", "seq", None), P("groups", "seq", None)),
        check_vma=False,
    )
```

```python
import functools

import jax
import jax.numpy as jnp
from jax import lax
from jax.experimental import pallas as pl
from jax.experimental.pallas import tpu as pltpu
from jax.sharding import PartitionSpec as P

HV = 32
HA = 16
HEAD = 128
PROMPTS = 4
MESH = pl.DeviceIdType.MESH
AHEAD = 2
JOIN = 1024
ROOM = 56 * 2**20


def attend(queries, key_rows, value_rows, bias):
    scores = lax.dot_general(
        queries, key_rows, (((1,), (1,)), ((), ())), preferred_element_type=jnp.float32
    ) * (HEAD**-0.5)
    if bias is not None:
        scores = scores + bias
    row_max = jnp.max(scores, axis=1, keepdims=True)
    weights = jnp.exp(scores - row_max)
    total = jnp.sum(weights, axis=1, keepdims=True)
    result = jnp.dot(
        weights.astype(jnp.bfloat16), value_rows, preferred_element_type=jnp.float32
    )
    return result / total, row_max + jnp.log(total)


def gate_of(branch_prompt, gates, branch, here):
    return sum(
        (branch_prompt[branch] == p).astype(jnp.int32).astype(jnp.float32)
        * gates[p : p + 1, here]
        for p in range(PROMPTS)
    )


def join_kernel(
    own_home,
    cross_home,
    audio_home,
    gates_far,
    prompt_far,
    video_out,
    audio_out,
    own,
    cross,
    audio,
    gates,
    branch_prompt,
    in_sems,
    out_sems,
    other_sems,
):
    branches, parts = own.shape[0], own.shape[2] // JOIN
    gate_copy = pltpu.make_async_copy(gates_far, gates, other_sems.at[0])
    prompt_copy = pltpu.make_async_copy(prompt_far, branch_prompt, other_sems.at[1])
    audio_in = pltpu.make_async_copy(audio_home, audio, other_sems.at[2])
    audio_away = pltpu.make_async_copy(audio, audio_out, other_sems.at[3])
    pieces = [
        (branch, slice(i * JOIN, (i + 1) * JOIN), branch * parts + i)
        for branch in range(branches)
        for i in range(parts)
    ]

    def came(branch, here, place):
        return (
            pltpu.make_async_copy(own_home.at[branch, :, here], own.at[branch, :, here], in_sems.at[place, 0]),
            pltpu.make_async_copy(
                cross_home.at[branch, :, here], cross.at[branch, :, here], in_sems.at[place, 1]
            ),
        )

    def goes(branch, here, place):
        return pltpu.make_async_copy(
            own.at[branch, :, here], video_out.at[branch, :, here], out_sems.at[place]
        )

    gate_copy.start()
    prompt_copy.start()
    for piece in pieces:
        for copy in came(*piece):
            copy.start()
    audio_in.start()
    gate_copy.wait()
    prompt_copy.wait()
    for branch, here, place in pieces:
        for copy in came(branch, here, place):
            copy.wait()
        own[branch, :, here] = (
            own[branch, :, here].astype(jnp.float32)
            + gate_of(branch_prompt, gates, branch, here) * cross[branch, :, here].astype(jnp.float32)
        ).astype(jnp.bfloat16)
        goes(branch, here, place).start()
    audio_in.wait()
    audio_away.start()
    for piece in pieces:
        goes(*piece).wait()
    audio_away.wait()


def block_kernel(
    n,
    video_outer,
    video_inner,
    cross_count,
    audio_outer,
    audio_inner,
    video_block,
    audio_block,
    video_qkv,
    video_q,
    audio_kv,
    audio_qkv,
    audio_q,
    video_kv,
    audio_gate_far,
    audio_valid_far,
    branch_prompt_far,
    own_home,
    cross_home,
    audio_out,
    audio_gate,
    audio_valid,
    branch_prompt,
    video_qkv_in,
    video_q_in,
    audio_kv_in,
    both_q_in,
    own_kv_in,
    video_kv_in,
    audio_pair,
    video_pair,
    video_res,
    cross_res,
    part_res,
    level_res,
    level_in,
    share_res,
    share_in,
    final_res,
    video_sems,
    cross_sems,
    both_sems,
    kv_sems,
    pair_sems,
    send_sems,
    back_sems,
    small_sems,
):
    me = lax.axis_index("seq")
    group = lax.axis_index("groups")
    video_local = own_home.shape[1]
    audio_local = audio_out.shape[1]

    barrier = pltpu.get_barrier_semaphore()

    def greet(k, carry):
        peer = lax.rem(me + k, n)
        pl.semaphore_signal(barrier, inc=1, device_id=(group, peer), device_id_type=MESH)
        return carry

    lax.fori_loop(1, n, greet, 0)
    small = [
        pltpu.make_async_copy(source, target, small_sems.at[i])
        for i, (source, target) in enumerate(
            (
                (audio_gate_far, audio_gate),
                (audio_valid_far, audio_valid),
                (branch_prompt_far, branch_prompt),
            )
        )
    ]
    for copy in small:
        copy.start()
    pl.semaphore_wait(barrier, n - 1)

    video_rows = pl.ds(pl.multiple_of(me * video_local, video_local), video_local)
    audio_rows = pl.ds(pl.multiple_of(me * audio_local, audio_local), audio_local)

    near, quarter = n // 2, n // 4
    my_half = me // near
    half_first = my_half * near
    place_in_half = me - half_first
    half_rows = pl.ds(pl.multiple_of(place_in_half * video_local, video_local), video_local)
    half_audio_rows = pl.ds(pl.multiple_of(place_in_half * audio_local, audio_local), audio_local)

    def is_inner(device):
        q = device // quarter
        return (q * (3 - q)) // 2

    inner = is_inner(me)
    outer_in_half = my_half * 3 * quarter

    def columns(head):
        return pl.ds(pl.multiple_of(head * HEAD, HEAD), HEAD)

    def video_place(device, slot):
        here = is_inner(device)
        high = device // near
        outside = (device - high * 2 * quarter) * video_outer + slot
        inside = 2 * quarter * video_outer + (device - quarter) * video_inner + slot
        item = outside + here * (inside - outside)
        return item // HV, lax.rem(item, HV)

    def cross_place(device, slot):
        item = lax.rem(device, near) * cross_count + slot
        return item // HV, lax.rem(item, HV)

    def audio_place(device, slot):
        here = is_inner(device)
        r = lax.rem(device, quarter)
        outside = r * audio_outer + slot
        inside = quarter * audio_outer + r * audio_inner + slot
        item = outside + here * (inside - outside)
        return item // HA, lax.rem(item, HA)

    def video_parts(peer, slot):
        branch, head = video_place(peer, slot)
        return (
            (
                video_qkv.at[branch, :, :, columns(head)],
                video_qkv_in.at[slot, :, video_rows],
                video_sems.at[slot],
            ),
        )

    def cross_q_parts(peer, slot):
        branch, head = cross_place(peer, slot)
        return (
            (
                video_q.at[branch, :, columns(head)],
                video_q_in.at[slot, half_rows],
                cross_sems.at[slot, 0],
            ),
        )

    def cross_kv_parts(peer, slot):
        branch, head = cross_place(peer, slot)
        return (
            (
                audio_kv.at[branch, :, :, columns(head)],
                audio_kv_in.at[slot, audio_rows],
                cross_sems.at[slot, 1],
            ),
        )

    def both_q_parts(peer, slot):
        branch, head = audio_place(peer, slot)
        return (
            (
                audio_qkv.at[branch, 0, :, columns(head)],
                both_q_in.at[slot, 0, audio_rows],
                both_sems.at[slot],
            ),
            (
                audio_q.at[branch, :, columns(head)],
                both_q_in.at[slot, 1, audio_rows],
                both_sems.at[slot],
            ),
        )

    def own_kv_parts(peer, slot):
        branch, head = audio_place(peer, slot)
        return (
            (
                audio_qkv.at[branch, 1:3, :, columns(head)],
                own_kv_in.at[slot, :, half_audio_rows],
                kv_sems.at[slot, 0],
            ),
        )

    def video_kv_parts(peer, slot):
        branch, head = audio_place(peer, slot)
        return (
            (
                video_kv.at[branch, :, :, columns(head)],
                video_kv_in.at[slot, half_rows],
                kv_sems.at[slot, 1],
            ),
        )

    def send(parts, slot, send_sem, first, span):
        place = lax.rem(me - first + n, n)
        member = 1 - jnp.minimum(place // span, 1)

        def to_peer(k, carry):
            step = k // 2 + lax.rem(k, 2) * (span // 2)
            peer = lax.rem(first + lax.rem(place + step, span), n)
            for source, target, sem in parts(peer, slot):
                pltpu.make_async_remote_copy(
                    src_ref=source,
                    dst_ref=target,
                    send_sem=send_sems.at[send_sem],
                    recv_sem=sem,
                    device_id=(group, peer),
                    device_id_type=MESH,
                ).start()
            return carry

        lax.fori_loop(member, span, to_peer, 0)

        @pl.when(member == 1)
        def _():
            for source, target, sem in parts(me, slot):
                pltpu.make_async_copy(source, target, sem).start()

    steps = video_inner + 1

    def cross_before(step):
        return (jnp.maximum(step, 1) - 1) * cross_count // (steps - 1)

    def send_step(step, carry):
        def send_cross(slot, inner_carry):
            send(cross_kv_parts, slot, 3, 0, n)
            send(cross_q_parts, slot, 2, half_first, near)
            return inner_carry

        lax.fori_loop(cross_before(step), cross_before(step + 1), send_cross, 0)
        @pl.when(step < video_outer)
        def _():
            send(video_parts, step, 0, 0, n)

        @pl.when((step >= video_outer) & (step < video_inner))
        def _():
            send(video_parts, step, 1, quarter, 2 * quarter)

        @pl.when(step < audio_inner)
        def _():
            send(both_q_parts, step, 4, 0, n)
            send(own_kv_parts, step, 6, half_first, near)
            send(video_kv_parts, step, 7, half_first, near)

        @pl.when((step >= audio_inner) & (step < audio_outer))
        def _():
            send(both_q_parts, step, 5, 3 * quarter, 2 * quarter)
            send(own_kv_parts, step, 8, outer_in_half, quarter)
            send(video_kv_parts, step, 9, outer_in_half, quarter)


        return carry

    lax.fori_loop(0, min(AHEAD, steps), send_step, 0)
    for copy in small:
        copy.wait()

    def mask(branch):
        positions = lax.broadcasted_iota(jnp.int32, (1, audio_kv_in.shape[1]), 1)
        return jnp.where(positions < audio_valid[branch], 0.0, -jnp.inf)

    def settle(ref, sem):
        pltpu.make_async_copy(ref, ref, sem).wait()

    def give_back(result, slot, out, branch, head, local, base, first, count, place):
        def to_peer(j, carry):
            peer = base + first + j
            source = result.at[slot, pl.ds(pl.multiple_of((first + j) * local, local), local)]
            target = out.at[branch, :, columns(head)]

            @pl.when(peer == me)
            def _():
                pltpu.make_async_copy(source, target, back_sems.at[place]).start()

            @pl.when(peer != me)
            def _():
                pltpu.make_async_remote_copy(
                    src_ref=source,
                    dst_ref=target,
                    send_sem=send_sems.at[10 + place],
                    recv_sem=back_sems.at[place],
                    device_id=(group, peer),
                    device_id_type=MESH,
                ).start()

            return carry

        lax.fori_loop(0, count, to_peer, 0)

    def part_kinds(source, slot, target):
        for first in range(0, target.shape[1], HEAD):
            here = slice(first, first + HEAD)
            target[:, here] = jnp.swapaxes(source[slot, here], 0, 1)

    def video_item(slot):
        branch, head = video_place(me, slot)
        settle(video_qkv_in.at[slot], video_sems.at[slot])
        block = video_block * video_local

        def rows(i, inner):
            here = pl.ds(pl.multiple_of(i * block, block), block)
            own, _ = attend(
                video_qkv_in[slot, 0, here], video_qkv_in[slot, 1], video_qkv_in[slot, 2], None
            )
            video_res[slot, here] = own.astype(jnp.bfloat16)
            give_back(
                video_res, slot, own_home, branch, head, video_local, 0, i * video_block,
                video_block, 0,
            )
            return inner

        lax.fori_loop(0, n // video_block, rows, 0)

    def cross_item(slot, carry):
        branch, head = cross_place(me, slot)
        settle(video_q_in.at[slot], cross_sems.at[slot, 0])
        settle(audio_kv_in.at[slot], cross_sems.at[slot, 1])
        part_kinds(audio_kv_in, slot, audio_pair)
        block = video_block * video_local

        def rows(i, inner):
            here = pl.ds(pl.multiple_of(i * block, block), block)
            cross, _ = attend(
                video_q_in[slot, here], audio_pair[0], audio_pair[1], mask(branch)
            )
            cross_res[slot, here] = cross.astype(jnp.bfloat16)
            give_back(
                cross_res, slot, cross_home, branch, head, video_local, half_first,
                i * video_block, video_block, 2,
            )
            return inner

        lax.fori_loop(0, near // video_block, rows, 0)
        return carry

    partner = (3 - me // quarter) * quarter + lax.rem(me, quarter)
    half_audio = near * audio_local
    chunks = n * audio_local // HEAD
    half_chunks = chunks // 2

    def half_mask(branch):
        positions = lax.broadcasted_iota(jnp.int32, (1, half_audio), 1) + my_half * half_audio
        return jnp.where(positions < audio_valid[branch], 0.0, -1e30)

    def to_partner(source, target, place, slot):
        pltpu.make_async_remote_copy(
            src_ref=source.at[slot],
            dst_ref=target.at[slot],
            send_sem=send_sems.at[13 + place],
            recv_sem=pair_sems.at[place, slot],
            device_id=(group, partner),
            device_id_type=MESH,
        ).start()

    def audio_item(slot):
        branch, head = audio_place(me, slot)
        settle(both_q_in.at[slot], both_sems.at[slot])
        settle(own_kv_in.at[slot], kv_sems.at[slot, 0])
        settle(video_kv_in.at[slot], kv_sems.at[slot, 1])
        part_kinds(video_kv_in, slot, video_pair)
        block = audio_block * audio_local
        per_block = block // HEAD

        def rows(i, inner):
            here = pl.ds(pl.multiple_of(i * block, block), block)
            for kind, (keys, bias) in enumerate(
                ((own_kv_in.at[slot], half_mask(branch)), (video_pair, None))
            ):
                part, level = attend(both_q_in[slot, kind, here], keys[0], keys[1], bias)
                part_res[slot, kind, here] = part
                for c in range(per_block):
                    column = jnp.broadcast_to(level[c * HEAD : (c + 1) * HEAD], (HEAD, HEAD))
                    level_res[slot, kind * chunks + i * per_block + c] = jnp.transpose(column)[0:1]
            return inner

        lax.fori_loop(0, n // audio_block, rows, 0)
        to_partner(level_res, level_in, 0, slot)

    def weighted(slot, chunk, gate):
        here = pl.ds(pl.multiple_of(chunk * HEAD, HEAD), HEAD)
        terms = []
        for kind in range(2):
            gap = level_in[slot, kind * chunks + chunk] - level_res[slot, kind * chunks + chunk]
            weight = jnp.transpose(jnp.broadcast_to(1.0 / (1.0 + jnp.exp(gap)), (HEAD, HEAD)))
            terms.append(weight * part_res[slot, kind, here])
        return terms[0] + gate * terms[1]

    def audio_share(slot):
        branch, head = audio_place(me, slot)
        settle(level_in.at[slot], pair_sems.at[0, slot])
        gate = gate_of(branch_prompt, audio_gate, branch, columns(head))
        for c in range(half_chunks):
            share_res[slot, c * HEAD : (c + 1) * HEAD] = weighted(
                slot, (1 - my_half) * half_chunks + c, gate
            ).astype(jnp.bfloat16)
        to_partner(share_res, share_in, 1, slot)

    def audio_final(slot):
        branch, head = audio_place(me, slot)
        settle(share_in.at[slot], pair_sems.at[1, slot])
        gate = gate_of(branch_prompt, audio_gate, branch, columns(head))
        for c in range(half_chunks):
            here = slice(c * HEAD, (c + 1) * HEAD)
            final_res[slot, here] = (
                weighted(slot, my_half * half_chunks + c, gate)
                + share_in[slot, here].astype(jnp.float32)
            ).astype(jnp.bfloat16)
        give_back(
            final_res, slot, audio_out, branch, head, audio_local, half_first, 0, near, 1
        )

    my_video = video_outer + inner * (video_inner - video_outer)
    my_audio = audio_outer + inner * (audio_inner - audio_outer)

    def work_step(step, carry):
        @pl.when(step + AHEAD < steps)
        def _():
            send_step(step + AHEAD, 0)

        @pl.when(step < my_audio)
        def _():
            audio_item(step)

        @pl.when(step < my_video)
        def _():
            video_item(step)

        @pl.when((step >= 1) & (step - 1 < my_audio))
        def _():
            audio_share(step - 1)

        lax.fori_loop(cross_before(step), cross_before(step + 1), cross_item, 0)

        @pl.when((step >= 2) & (step - 2 < my_audio))
        def _():
            audio_final(step - 2)

        return carry

    lax.fori_loop(0, steps, work_step, 0)

    @pl.when(my_audio == steps - 1)
    def _():
        audio_final(steps - 2)

    settle(own_home, back_sems.at[0])
    settle(cross_home, back_sems.at[2])
    settle(audio_out, back_sems.at[1])

    far_half = pl.ds(0, (near - 1) * video_local)
    far_video = pl.ds(0, (n - 1) * video_local)

    def few(count, local):
        return pl.ds(0, count * local)

    settle(video_qkv_in.at[0:video_outer, :, far_video], send_sems.at[0])
    settle(video_q_in.at[:, far_half], send_sems.at[2])
    settle(audio_kv_in.at[:, few(n - 1, audio_local)], send_sems.at[3])
    settle(both_q_in.at[0:audio_inner, :, few(n - 1, audio_local)], send_sems.at[4])
    settle(own_kv_in.at[0:audio_inner, :, few(near - 1, audio_local)], send_sems.at[6])
    settle(video_kv_in.at[0:audio_inner, far_half], send_sems.at[7])
    settle(cross_res.at[:, far_half], send_sems.at[12])

    for here in range(2):

        @pl.when(inner == here)
        def _():
            away = 1 - here
            more_video = pl.ds(video_outer, video_inner - video_outer)
            more_audio = pl.ds(audio_inner, audio_outer - audio_inner)
            videos = pl.ds(0, (video_outer, video_inner)[here])
            audios = pl.ds(0, (audio_outer, audio_inner)[here])
            settle(video_qkv_in.at[more_video, :, few(2 * quarter - here, video_local)], send_sems.at[1])
            settle(both_q_in.at[more_audio, :, few(2 * quarter - away, audio_local)], send_sems.at[5])
            settle(own_kv_in.at[more_audio, :, few(quarter - away, audio_local)], send_sems.at[8])
            settle(video_kv_in.at[more_audio, few(quarter - away, video_local)], send_sems.at[9])
            settle(video_res.at[videos, far_video], send_sems.at[10])
            settle(final_res.at[audios, few(near - 1, audio_local)], send_sems.at[11])
            settle(level_res.at[audios], send_sems.at[13])
            settle(share_res.at[audios], send_sems.at[14])


def kinds_first(source):
    return jnp.transpose(source, (0, 2, 1, 3))


def shares(total):
    return total // 4, total - total // 4


def on_device(
    n,
    video_qkv,
    video_cross_q,
    audio_kv_v,
    audio_qkv,
    audio_cross_q,
    video_kv_a,
    audio_valid,
    branch_prompt,
    video_gate,
    audio_gate,
):
    branches, video_local = video_cross_q.shape[:2]
    audio_local = audio_cross_q.shape[1]
    video_all, audio_all = video_local * n, audio_local * n
    near, quarter = n // 2, n // 4
    video_outer, video_inner = shares(branches * HV // near)
    cross_count = branches * HV // near
    audio_inner, audio_outer = shares(branches * HA // quarter)
    hbm = pl.BlockSpec(memory_space=pltpu.HBM)
    half = jnp.bfloat16
    pieces = branches * video_cross_q.shape[2] // JOIN
    homes = pl.pallas_call(
        functools.partial(
            block_kernel,
            n,
            video_outer,
            video_inner,
            cross_count,
            audio_outer,
            audio_inner,
            min(4, near),
            min(8, n),
        ),
        out_shape=(
            jax.ShapeDtypeStruct(video_cross_q.shape, half),
            jax.ShapeDtypeStruct(video_cross_q.shape, half),
            jax.ShapeDtypeStruct(audio_cross_q.shape, half),
        ),
        in_specs=[hbm] * 9,
        out_specs=(hbm,) * 3,
        scratch_shapes=[
            pltpu.VMEM(audio_gate.shape, jnp.float32),
            pltpu.SMEM(audio_valid.shape, jnp.int32),
            pltpu.SMEM(branch_prompt.shape, jnp.int32),
            pltpu.VMEM((video_inner, 3, video_all, HEAD), half),
            pltpu.VMEM((cross_count, near * video_local, HEAD), half),
            pltpu.VMEM((cross_count, audio_all, 2, HEAD), half),
            pltpu.VMEM((audio_outer, 2, audio_all, HEAD), half),
            pltpu.VMEM((audio_outer, 2, near * audio_local, HEAD), half),
            pltpu.VMEM((audio_outer, near * video_local, 2, HEAD), half),
            pltpu.VMEM((2, audio_all, HEAD), half),
            pltpu.VMEM((2, near * video_local, HEAD), half),
            pltpu.VMEM((video_inner, video_all, HEAD), half),
            pltpu.VMEM((cross_count, near * video_local, HEAD), half),
            pltpu.VMEM((audio_outer, 2, audio_all, HEAD), jnp.float32),
            pltpu.VMEM((audio_outer, 2 * audio_all // HEAD, 1, HEAD), jnp.float32),
            pltpu.VMEM((audio_outer, 2 * audio_all // HEAD, 1, HEAD), jnp.float32),
            pltpu.VMEM((audio_outer, near * audio_local, HEAD), half),
            pltpu.VMEM((audio_outer, near * audio_local, HEAD), half),
            pltpu.VMEM((audio_outer, near * audio_local, HEAD), half),
            pltpu.SemaphoreType.DMA((video_inner,)),
            pltpu.SemaphoreType.DMA((cross_count, 2)),
            pltpu.SemaphoreType.DMA((audio_outer,)),
            pltpu.SemaphoreType.DMA((audio_outer, 2)),
            pltpu.SemaphoreType.DMA((2, audio_outer)),
            pltpu.SemaphoreType.DMA((15,)),
            pltpu.SemaphoreType.DMA((3,)),
            pltpu.SemaphoreType.DMA((3,)),
        ],
        compiler_params=pltpu.CompilerParams(
            collective_id=0, has_side_effects=True, vmem_limit_bytes=ROOM
        ),
    )(
        kinds_first(video_qkv),
        video_cross_q,
        audio_kv_v,
        kinds_first(audio_qkv),
        audio_cross_q,
        video_kv_a,
        audio_gate,
        audio_valid,
        branch_prompt,
    )
    return tuple(
        pl.pallas_call(
            join_kernel,
            out_shape=(
                jax.ShapeDtypeStruct(video_cross_q.shape, half),
                jax.ShapeDtypeStruct(audio_cross_q.shape, half),
            ),
            in_specs=[hbm] * 5,
            out_specs=(hbm, hbm),
            scratch_shapes=[
                pltpu.VMEM(video_cross_q.shape, half),
                pltpu.VMEM(video_cross_q.shape, half),
                pltpu.VMEM(audio_cross_q.shape, half),
                pltpu.VMEM(video_gate.shape, jnp.float32),
                pltpu.SMEM(branch_prompt.shape, jnp.int32),
                pltpu.SemaphoreType.DMA((pieces, 2)),
                pltpu.SemaphoreType.DMA((pieces,)),
                pltpu.SemaphoreType.DMA((4,)),
            ],
            compiler_params=pltpu.CompilerParams(vmem_limit_bytes=ROOM),
        )(*homes, video_gate, branch_prompt)
    )


def solution(mesh):
    placed = (
        P("groups", "seq", None, None),
        P("groups", "seq", None),
        P("groups", "seq", None, None),
        P("groups", "seq", None, None),
        P("groups", "seq", None),
        P("groups", "seq", None, None),
        P("groups"),
        P("groups"),
        P(),
        P(),
    )
    return jax.shard_map(
        functools.partial(on_device, mesh.shape["seq"]),
        mesh=mesh,
        in_specs=placed,
        out_specs=(P("groups", "seq", None), P("groups", "seq", None)),
        check_vma=False,
    )
```

```python
import functools

import jax
import jax.numpy as jnp
from jax import lax
from jax.experimental import pallas as pl
from jax.experimental.pallas import tpu as pltpu
from jax.sharding import PartitionSpec as P

HV = 32
HA = 16
HEAD = 128
PROMPTS = 4
MESH = pl.DeviceIdType.MESH
AHEAD = 2
JOIN = 1024
ROOM = 56 * 2**20


def attend(queries, key_rows, value_rows, bias):
    scores = lax.dot_general(
        queries, key_rows, (((1,), (1,)), ((), ())), preferred_element_type=jnp.float32
    ) * (HEAD**-0.5)
    if bias is not None:
        scores = scores + bias
    row_max = jnp.max(scores, axis=1, keepdims=True)
    weights = jnp.exp(scores - row_max)
    total = jnp.sum(weights, axis=1, keepdims=True)
    result = jnp.dot(
        weights.astype(jnp.bfloat16), value_rows, preferred_element_type=jnp.float32
    )
    return result / total, row_max + jnp.log(total)


def gate_of(branch_prompt, gates, branch, here):
    return sum(
        (branch_prompt[branch] == p).astype(jnp.int32).astype(jnp.float32)
        * gates[p : p + 1, here]
        for p in range(PROMPTS)
    )


def join_kernel(
    own_home,
    cross_home,
    audio_home,
    gates_far,
    prompt_far,
    video_out,
    audio_out,
    own,
    cross,
    audio,
    gates,
    branch_prompt,
    in_sems,
    out_sems,
    other_sems,
):
    branches, parts = own.shape[0], own.shape[2] // JOIN
    gate_copy = pltpu.make_async_copy(gates_far, gates, other_sems.at[0])
    prompt_copy = pltpu.make_async_copy(prompt_far, branch_prompt, other_sems.at[1])
    audio_in = pltpu.make_async_copy(audio_home, audio, other_sems.at[2])
    audio_away = pltpu.make_async_copy(audio, audio_out, other_sems.at[3])
    pieces = [
        (branch, slice(i * JOIN, (i + 1) * JOIN), branch * parts + i)
        for branch in range(branches)
        for i in range(parts)
    ]

    def came(branch, here, place):
        return (
            pltpu.make_async_copy(own_home.at[branch, :, here], own.at[branch, :, here], in_sems.at[place, 0]),
            pltpu.make_async_copy(
                cross_home.at[branch, :, here], cross.at[branch, :, here], in_sems.at[place, 1]
            ),
        )

    def goes(branch, here, place):
        return pltpu.make_async_copy(
            own.at[branch, :, here], video_out.at[branch, :, here], out_sems.at[place]
        )

    gate_copy.start()
    prompt_copy.start()
    for piece in pieces:
        for copy in came(*piece):
            copy.start()
    audio_in.start()
    gate_copy.wait()
    prompt_copy.wait()
    for branch, here, place in pieces:
        for copy in came(branch, here, place):
            copy.wait()
        own[branch, :, here] = (
            own[branch, :, here].astype(jnp.float32)
            + gate_of(branch_prompt, gates, branch, here) * cross[branch, :, here].astype(jnp.float32)
        ).astype(jnp.bfloat16)
        goes(branch, here, place).start()
    audio_in.wait()
    audio_away.start()
    for piece in pieces:
        goes(*piece).wait()
    audio_away.wait()


def block_kernel(
    n,
    video_outer,
    video_inner,
    cross_count,
    audio_outer,
    audio_inner,
    video_block,
    audio_block,
    video_qkv,
    video_q,
    audio_kv,
    audio_qkv,
    audio_q,
    video_kv,
    audio_gate_far,
    audio_valid_far,
    branch_prompt_far,
    own_home,
    cross_home,
    audio_out,
    audio_gate,
    audio_valid,
    branch_prompt,
    video_qkv_in,
    video_q_in,
    audio_kv_in,
    both_q_in,
    own_kv_in,
    video_kv_in,
    audio_pair,
    video_pair,
    video_res,
    cross_res,
    part_res,
    level_res,
    level_in,
    share_res,
    share_in,
    final_res,
    video_sems,
    cross_sems,
    both_sems,
    kv_sems,
    pair_sems,
    send_sems,
    back_sems,
    small_sems,
):
    me = lax.axis_index("seq")
    group = lax.axis_index("groups")
    video_local = own_home.shape[1]
    audio_local = audio_out.shape[1]

    barrier = pltpu.get_barrier_semaphore()

    def greet(k, carry):
        peer = lax.rem(me + k, n)
        pl.semaphore_signal(barrier, inc=1, device_id=(group, peer), device_id_type=MESH)
        return carry

    lax.fori_loop(1, n, greet, 0)
    small = [
        pltpu.make_async_copy(source, target, small_sems.at[i])
        for i, (source, target) in enumerate(
            (
                (audio_gate_far, audio_gate),
                (audio_valid_far, audio_valid),
                (branch_prompt_far, branch_prompt),
            )
        )
    ]
    for copy in small:
        copy.start()
    pl.semaphore_wait(barrier, n - 1)

    video_rows = pl.ds(pl.multiple_of(me * video_local, video_local), video_local)
    audio_rows = pl.ds(pl.multiple_of(me * audio_local, audio_local), audio_local)

    near, quarter = n // 2, n // 4
    my_half = me // near
    half_first = my_half * near
    place_in_half = me - half_first
    half_rows = pl.ds(pl.multiple_of(place_in_half * video_local, video_local), video_local)
    half_audio_rows = pl.ds(pl.multiple_of(place_in_half * audio_local, audio_local), audio_local)

    def is_inner(device):
        q = device // quarter
        return (q * (3 - q)) // 2

    inner = is_inner(me)
    outer_in_half = my_half * 3 * quarter

    def columns(head):
        return pl.ds(pl.multiple_of(head * HEAD, HEAD), HEAD)

    def video_place(device, slot):
        here = is_inner(device)
        high = device // near
        outside = (device - high * 2 * quarter) * video_outer + slot
        inside = 2 * quarter * video_outer + (device - quarter) * video_inner + slot
        item = outside + here * (inside - outside)
        return item // HV, lax.rem(item, HV)

    def cross_place(device, slot):
        item = lax.rem(device, near) * cross_count + slot
        return item // HV, lax.rem(item, HV)

    def audio_place(device, slot):
        here = is_inner(device)
        r = lax.rem(device, quarter)
        outside = r * audio_outer + slot
        inside = quarter * audio_outer + r * audio_inner + slot
        item = outside + here * (inside - outside)
        return item // HA, lax.rem(item, HA)

    def video_parts(peer, slot):
        branch, head = video_place(peer, slot)
        return (
            (
                video_qkv.at[branch, :, :, columns(head)],
                video_qkv_in.at[slot, :, video_rows],
                video_sems.at[slot],
            ),
        )

    def cross_q_parts(peer, slot):
        branch, head = cross_place(peer, slot)
        return (
            (
                video_q.at[branch, :, columns(head)],
                video_q_in.at[slot, half_rows],
                cross_sems.at[slot, 0],
            ),
        )

    def cross_kv_parts(peer, slot):
        branch, head = cross_place(peer, slot)
        return (
            (
                audio_kv.at[branch, :, :, columns(head)],
                audio_kv_in.at[slot, audio_rows],
                cross_sems.at[slot, 1],
            ),
        )

    def both_q_parts(peer, slot):
        branch, head = audio_place(peer, slot)
        return (
            (
                audio_qkv.at[branch, 0, :, columns(head)],
                both_q_in.at[slot, 0, audio_rows],
                both_sems.at[slot],
            ),
            (
                audio_q.at[branch, :, columns(head)],
                both_q_in.at[slot, 1, audio_rows],
                both_sems.at[slot],
            ),
        )

    def own_kv_parts(peer, slot):
        branch, head = audio_place(peer, slot)
        return (
            (
                audio_qkv.at[branch, 1:3, :, columns(head)],
                own_kv_in.at[slot, :, half_audio_rows],
                kv_sems.at[slot, 0],
            ),
        )

    def video_kv_parts(peer, slot):
        branch, head = audio_place(peer, slot)
        return (
            (
                video_kv.at[branch, :, :, columns(head)],
                video_kv_in.at[slot, half_rows],
                kv_sems.at[slot, 1],
            ),
        )

    def send(parts, slot, send_sem, first, span):
        place = lax.rem(me - first + n, n)
        member = 1 - jnp.minimum(place // span, 1)

        def to_peer(k, carry):
            step = k // 2 + lax.rem(k, 2) * (span // 2)
            peer = lax.rem(first + lax.rem(place + step, span), n)
            for source, target, sem in parts(peer, slot):
                pltpu.make_async_remote_copy(
                    src_ref=source,
                    dst_ref=target,
                    send_sem=send_sems.at[send_sem],
                    recv_sem=sem,
                    device_id=(group, peer),
                    device_id_type=MESH,
                ).start()
            return carry

        lax.fori_loop(member, span, to_peer, 0)

        @pl.when(member == 1)
        def _():
            for source, target, sem in parts(me, slot):
                pltpu.make_async_copy(source, target, sem).start()

    steps = video_inner + 1

    def cross_before(step):
        return step * cross_count // steps

    def send_step(step, carry):
        def send_cross(slot, inner_carry):
            send(cross_kv_parts, slot, 3, 0, n)
            send(cross_q_parts, slot, 2, half_first, near)
            return inner_carry

        lax.fori_loop(cross_before(step), cross_before(step + 1), send_cross, 0)
        @pl.when(step < video_outer)
        def _():
            send(video_parts, step, 0, 0, n)

        @pl.when((step >= video_outer) & (step < video_inner))
        def _():
            send(video_parts, step, 1, quarter, 2 * quarter)

        @pl.when(step < audio_inner)
        def _():
            send(both_q_parts, step, 4, 0, n)
            send(own_kv_parts, step, 6, half_first, near)
            send(video_kv_parts, step, 7, half_first, near)

        @pl.when((step >= audio_inner) & (step < audio_outer))
        def _():
            send(both_q_parts, step, 5, 3 * quarter, 2 * quarter)
            send(own_kv_parts, step, 8, outer_in_half, quarter)
            send(video_kv_parts, step, 9, outer_in_half, quarter)


        return carry

    lax.fori_loop(0, min(AHEAD, steps), send_step, 0)
    for copy in small:
        copy.wait()

    def mask(branch):
        positions = lax.broadcasted_iota(jnp.int32, (1, audio_kv_in.shape[1]), 1)
        return jnp.where(positions < audio_valid[branch], 0.0, -jnp.inf)

    def settle(ref, sem):
        pltpu.make_async_copy(ref, ref, sem).wait()

    def give_back(result, slot, out, branch, head, local, base, first, count, place):
        def to_peer(j, carry):
            peer = base + first + j
            source = result.at[slot, pl.ds(pl.multiple_of((first + j) * local, local), local)]
            target = out.at[branch, :, columns(head)]

            @pl.when(peer == me)
            def _():
                pltpu.make_async_copy(source, target, back_sems.at[place]).start()

            @pl.when(peer != me)
            def _():
                pltpu.make_async_remote_copy(
                    src_ref=source,
                    dst_ref=target,
                    send_sem=send_sems.at[10 + place],
                    recv_sem=back_sems.at[place],
                    device_id=(group, peer),
                    device_id_type=MESH,
                ).start()

            return carry

        lax.fori_loop(0, count, to_peer, 0)

    def part_kinds(source, slot, target):
        for first in range(0, target.shape[1], HEAD):
            here = slice(first, first + HEAD)
            target[:, here] = jnp.swapaxes(source[slot, here], 0, 1)

    def video_item(slot):
        branch, head = video_place(me, slot)
        settle(video_qkv_in.at[slot], video_sems.at[slot])
        block = video_block * video_local

        def rows(i, inner):
            here = pl.ds(pl.multiple_of(i * block, block), block)
            own, _ = attend(
                video_qkv_in[slot, 0, here], video_qkv_in[slot, 1], video_qkv_in[slot, 2], None
            )
            video_res[slot, here] = own.astype(jnp.bfloat16)
            give_back(
                video_res, slot, own_home, branch, head, video_local, 0, i * video_block,
                video_block, 0,
            )
            return inner

        lax.fori_loop(0, n // video_block, rows, 0)

    def cross_item(slot, carry):
        branch, head = cross_place(me, slot)
        settle(video_q_in.at[slot], cross_sems.at[slot, 0])
        settle(audio_kv_in.at[slot], cross_sems.at[slot, 1])
        part_kinds(audio_kv_in, slot, audio_pair)
        block = video_block * video_local

        def rows(i, inner):
            here = pl.ds(pl.multiple_of(i * block, block), block)
            cross, _ = attend(
                video_q_in[slot, here], audio_pair[0], audio_pair[1], mask(branch)
            )
            cross_res[slot, here] = cross.astype(jnp.bfloat16)
            give_back(
                cross_res, slot, cross_home, branch, head, video_local, half_first,
                i * video_block, video_block, 2,
            )
            return inner

        lax.fori_loop(0, near // video_block, rows, 0)
        return carry

    partner = (3 - me // quarter) * quarter + lax.rem(me, quarter)
    half_audio = near * audio_local
    chunks = n * audio_local // HEAD
    half_chunks = chunks // 2

    def half_mask(branch):
        positions = lax.broadcasted_iota(jnp.int32, (1, half_audio), 1) + my_half * half_audio
        return jnp.where(positions < audio_valid[branch], 0.0, -1e30)

    def to_partner(source, target, place, slot):
        pltpu.make_async_remote_copy(
            src_ref=source.at[slot],
            dst_ref=target.at[slot],
            send_sem=send_sems.at[13 + place],
            recv_sem=pair_sems.at[place, slot],
            device_id=(group, partner),
            device_id_type=MESH,
        ).start()

    def audio_item(slot):
        branch, head = audio_place(me, slot)
        settle(both_q_in.at[slot], both_sems.at[slot])
        settle(own_kv_in.at[slot], kv_sems.at[slot, 0])
        settle(video_kv_in.at[slot], kv_sems.at[slot, 1])
        part_kinds(video_kv_in, slot, video_pair)
        block = audio_block * audio_local
        per_block = block // HEAD

        def rows(i, inner):
            here = pl.ds(pl.multiple_of(i * block, block), block)
            for kind, (keys, bias) in enumerate(
                ((own_kv_in.at[slot], half_mask(branch)), (video_pair, None))
            ):
                part, level = attend(both_q_in[slot, kind, here], keys[0], keys[1], bias)
                part_res[slot, kind, here] = part
                for c in range(per_block):
                    column = jnp.broadcast_to(level[c * HEAD : (c + 1) * HEAD], (HEAD, HEAD))
                    level_res[slot, kind * chunks + i * per_block + c] = jnp.transpose(column)[0:1]
            return inner

        lax.fori_loop(0, n // audio_block, rows, 0)
        to_partner(level_res, level_in, 0, slot)

    def weighted(slot, chunk, gate):
        here = pl.ds(pl.multiple_of(chunk * HEAD, HEAD), HEAD)
        terms = []
        for kind in range(2):
            gap = level_in[slot, kind * chunks + chunk] - level_res[slot, kind * chunks + chunk]
            weight = jnp.transpose(jnp.broadcast_to(1.0 / (1.0 + jnp.exp(gap)), (HEAD, HEAD)))
            terms.append(weight * part_res[slot, kind, here])
        return terms[0] + gate * terms[1]

    def audio_share(slot):
        branch, head = audio_place(me, slot)
        settle(level_in.at[slot], pair_sems.at[0, slot])
        gate = gate_of(branch_prompt, audio_gate, branch, columns(head))
        for c in range(half_chunks):
            share_res[slot, c * HEAD : (c + 1) * HEAD] = weighted(
                slot, (1 - my_half) * half_chunks + c, gate
            ).astype(jnp.bfloat16)
        to_partner(share_res, share_in, 1, slot)

    def audio_final(slot):
        branch, head = audio_place(me, slot)
        settle(share_in.at[slot], pair_sems.at[1, slot])
        gate = gate_of(branch_prompt, audio_gate, branch, columns(head))
        for c in range(half_chunks):
            here = slice(c * HEAD, (c + 1) * HEAD)
            final_res[slot, here] = (
                weighted(slot, my_half * half_chunks + c, gate)
                + share_in[slot, here].astype(jnp.float32)
            ).astype(jnp.bfloat16)
        give_back(
            final_res, slot, audio_out, branch, head, audio_local, half_first, 0, near, 1
        )

    my_video = video_outer + inner * (video_inner - video_outer)
    my_audio = audio_outer + inner * (audio_inner - audio_outer)

    def work_step(step, carry):
        @pl.when(step + AHEAD < steps)
        def _():
            send_step(step + AHEAD, 0)

        @pl.when(step < my_audio)
        def _():
            audio_item(step)

        @pl.when(step < my_video)
        def _():
            video_item(step)

        @pl.when((step >= 1) & (step - 1 < my_audio))
        def _():
            audio_share(step - 1)

        lax.fori_loop(cross_before(step), cross_before(step + 1), cross_item, 0)

        @pl.when((step >= 2) & (step - 2 < my_audio))
        def _():
            audio_final(step - 2)

        return carry

    lax.fori_loop(0, steps, work_step, 0)

    @pl.when(my_audio == steps - 1)
    def _():
        audio_final(steps - 2)

    settle(own_home, back_sems.at[0])
    settle(cross_home, back_sems.at[2])
    settle(audio_out, back_sems.at[1])

    far_half = pl.ds(0, (near - 1) * video_local)
    far_video = pl.ds(0, (n - 1) * video_local)

    def few(count, local):
        return pl.ds(0, count * local)

    settle(video_qkv_in.at[0:video_outer, :, far_video], send_sems.at[0])
    settle(video_q_in.at[:, far_half], send_sems.at[2])
    settle(audio_kv_in.at[:, few(n - 1, audio_local)], send_sems.at[3])
    settle(both_q_in.at[0:audio_inner, :, few(n - 1, audio_local)], send_sems.at[4])
    settle(own_kv_in.at[0:audio_inner, :, few(near - 1, audio_local)], send_sems.at[6])
    settle(video_kv_in.at[0:audio_inner, far_half], send_sems.at[7])
    settle(cross_res.at[:, far_half], send_sems.at[12])

    for here in range(2):

        @pl.when(inner == here)
        def _():
            away = 1 - here
            more_video = pl.ds(video_outer, video_inner - video_outer)
            more_audio = pl.ds(audio_inner, audio_outer - audio_inner)
            videos = pl.ds(0, (video_outer, video_inner)[here])
            audios = pl.ds(0, (audio_outer, audio_inner)[here])
            settle(video_qkv_in.at[more_video, :, few(2 * quarter - here, video_local)], send_sems.at[1])
            settle(both_q_in.at[more_audio, :, few(2 * quarter - away, audio_local)], send_sems.at[5])
            settle(own_kv_in.at[more_audio, :, few(quarter - away, audio_local)], send_sems.at[8])
            settle(video_kv_in.at[more_audio, few(quarter - away, video_local)], send_sems.at[9])
            settle(video_res.at[videos, far_video], send_sems.at[10])
            settle(final_res.at[audios, few(near - 1, audio_local)], send_sems.at[11])
            settle(level_res.at[audios], send_sems.at[13])
            settle(share_res.at[audios], send_sems.at[14])


def kinds_first(source):
    return jnp.transpose(source, (0, 2, 1, 3))


def shares(total):
    return total // 4, total - total // 4


def on_device(
    n,
    video_qkv,
    video_cross_q,
    audio_kv_v,
    audio_qkv,
    audio_cross_q,
    video_kv_a,
    audio_valid,
    branch_prompt,
    video_gate,
    audio_gate,
):
    branches, video_local = video_cross_q.shape[:2]
    audio_local = audio_cross_q.shape[1]
    video_all, audio_all = video_local * n, audio_local * n
    near, quarter = n // 2, n // 4
    video_outer, video_inner = shares(branches * HV // near)
    cross_count = branches * HV // near
    audio_inner, audio_outer = shares(branches * HA // quarter)
    hbm = pl.BlockSpec(memory_space=pltpu.HBM)
    half = jnp.bfloat16
    pieces = branches * video_cross_q.shape[2] // JOIN
    homes = pl.pallas_call(
        functools.partial(
            block_kernel,
            n,
            video_outer,
            video_inner,
            cross_count,
            audio_outer,
            audio_inner,
            min(4, near),
            min(8, n),
        ),
        out_shape=(
            jax.ShapeDtypeStruct(video_cross_q.shape, half),
            jax.ShapeDtypeStruct(video_cross_q.shape, half),
            jax.ShapeDtypeStruct(audio_cross_q.shape, half),
        ),
        in_specs=[hbm] * 9,
        out_specs=(hbm,) * 3,
        scratch_shapes=[
            pltpu.VMEM(audio_gate.shape, jnp.float32),
            pltpu.SMEM(audio_valid.shape, jnp.int32),
            pltpu.SMEM(branch_prompt.shape, jnp.int32),
            pltpu.VMEM((video_inner, 3, video_all, HEAD), half),
            pltpu.VMEM((cross_count, near * video_local, HEAD), half),
            pltpu.VMEM((cross_count, audio_all, 2, HEAD), half),
            pltpu.VMEM((audio_outer, 2, audio_all, HEAD), half),
            pltpu.VMEM((audio_outer, 2, near * audio_local, HEAD), half),
            pltpu.VMEM((audio_outer, near * video_local, 2, HEAD), half),
            pltpu.VMEM((2, audio_all, HEAD), half),
            pltpu.VMEM((2, near * video_local, HEAD), half),
            pltpu.VMEM((video_inner, video_all, HEAD), half),
            pltpu.VMEM((cross_count, near * video_local, HEAD), half),
            pltpu.VMEM((audio_outer, 2, audio_all, HEAD), jnp.float32),
            pltpu.VMEM((audio_outer, 2 * audio_all // HEAD, 1, HEAD), jnp.float32),
            pltpu.VMEM((audio_outer, 2 * audio_all // HEAD, 1, HEAD), jnp.float32),
            pltpu.VMEM((audio_outer, near * audio_local, HEAD), half),
            pltpu.VMEM((audio_outer, near * audio_local, HEAD), half),
            pltpu.VMEM((audio_outer, near * audio_local, HEAD), half),
            pltpu.SemaphoreType.DMA((video_inner,)),
            pltpu.SemaphoreType.DMA((cross_count, 2)),
            pltpu.SemaphoreType.DMA((audio_outer,)),
            pltpu.SemaphoreType.DMA((audio_outer, 2)),
            pltpu.SemaphoreType.DMA((2, audio_outer)),
            pltpu.SemaphoreType.DMA((15,)),
            pltpu.SemaphoreType.DMA((3,)),
            pltpu.SemaphoreType.DMA((3,)),
        ],
        compiler_params=pltpu.CompilerParams(
            collective_id=0, has_side_effects=True, vmem_limit_bytes=ROOM
        ),
    )(
        kinds_first(video_qkv),
        video_cross_q,
        audio_kv_v,
        kinds_first(audio_qkv),
        audio_cross_q,
        video_kv_a,
        audio_gate,
        audio_valid,
        branch_prompt,
    )
    return tuple(
        pl.pallas_call(
            join_kernel,
            out_shape=(
                jax.ShapeDtypeStruct(video_cross_q.shape, half),
                jax.ShapeDtypeStruct(audio_cross_q.shape, half),
            ),
            in_specs=[hbm] * 5,
            out_specs=(hbm, hbm),
            scratch_shapes=[
                pltpu.VMEM(video_cross_q.shape, half),
                pltpu.VMEM(video_cross_q.shape, half),
                pltpu.VMEM(audio_cross_q.shape, half),
                pltpu.VMEM(video_gate.shape, jnp.float32),
                pltpu.SMEM(branch_prompt.shape, jnp.int32),
                pltpu.SemaphoreType.DMA((pieces, 2)),
                pltpu.SemaphoreType.DMA((pieces,)),
                pltpu.SemaphoreType.DMA((4,)),
            ],
            compiler_params=pltpu.CompilerParams(vmem_limit_bytes=ROOM),
        )(*homes, video_gate, branch_prompt)
    )


def solution(mesh):
    placed = (
        P("groups", "seq", None, None),
        P("groups", "seq", None),
        P("groups", "seq", None, None),
        P("groups", "seq", None, None),
        P("groups", "seq", None),
        P("groups", "seq", None, None),
        P("groups"),
        P("groups"),
        P(),
        P(),
    )
    return jax.shard_map(
        functools.partial(on_device, mesh.shape["seq"]),
        mesh=mesh,
        in_specs=placed,
        out_specs=(P("groups", "seq", None), P("groups", "seq", None)),
        check_vma=False,
    )
```

```python
import functools

import jax
import jax.numpy as jnp
from jax import lax
from jax.experimental import pallas as pl
from jax.experimental.pallas import tpu as pltpu
from jax.sharding import PartitionSpec as P

HV = 32
HA = 16
HEAD = 128
PROMPTS = 4
MESH = pl.DeviceIdType.MESH
AHEAD = 2
JOIN = 1024


def attend(queries, key_rows, value_rows, bias):
    scores = lax.dot_general(
        queries, key_rows, (((1,), (1,)), ((), ())), preferred_element_type=jnp.float32
    ) * (HEAD**-0.5)
    if bias is not None:
        scores = scores + bias
    row_max = jnp.max(scores, axis=1, keepdims=True)
    weights = jnp.exp(scores - row_max)
    total = jnp.sum(weights, axis=1, keepdims=True)
    result = jnp.dot(
        weights.astype(jnp.bfloat16), value_rows, preferred_element_type=jnp.float32
    )
    return result / total, row_max + jnp.log(total)


def gate_of(branch_prompt, gates, branch, here):
    return sum(
        (branch_prompt[branch] == p).astype(jnp.int32).astype(jnp.float32)
        * gates[p : p + 1, here]
        for p in range(PROMPTS)
    )


def join_kernel(
    own_home, cross_home, audio_home, video_gates, video_out, audio_out, joined, sems
):
    width = JOIN
    branches, parts = own_home.shape[0], own_home.shape[2] // width
    audio = pltpu.make_async_copy(audio_home, audio_out, sems.at[branches * parts])
    audio.start()
    for branch in range(branches):
        for i in range(parts):
            here = slice(i * width, (i + 1) * width)
            joined[branch, :, here] = (
                own_home[branch, :, here].astype(jnp.float32)
                + video_gates[branch : branch + 1, here]
                * cross_home[branch, :, here].astype(jnp.float32)
            ).astype(jnp.bfloat16)
            pltpu.make_async_copy(
                joined.at[branch, :, here], video_out.at[branch, :, here], sems.at[branch * parts + i]
            ).start()
    for branch in range(branches):
        for i in range(parts):
            here = slice(i * width, (i + 1) * width)
            pltpu.make_async_copy(
                joined.at[branch, :, here], video_out.at[branch, :, here], sems.at[branch * parts + i]
            ).wait()
    audio.wait()


def block_kernel(
    n,
    video_outer,
    video_inner,
    cross_count,
    audio_outer,
    audio_inner,
    video_block,
    audio_block,
    video_qkv,
    video_q,
    audio_kv,
    audio_qkv,
    audio_q,
    video_kv,
    video_gate_far,
    audio_gate_far,
    audio_valid_far,
    branch_prompt_far,
    own_home,
    cross_home,
    audio_out,
    video_gates,
    video_gate,
    audio_gate,
    audio_valid,
    branch_prompt,
    video_qkv_in,
    video_q_in,
    audio_kv_in,
    both_q_in,
    own_kv_in,
    video_kv_in,
    audio_pair,
    video_pair,
    video_res,
    cross_res,
    part_res,
    level_res,
    level_in,
    share_res,
    share_in,
    final_res,
    video_sems,
    cross_sems,
    both_sems,
    kv_sems,
    pair_sems,
    send_sems,
    back_sems,
    small_sems,
):
    me = lax.axis_index("seq")
    group = lax.axis_index("groups")
    video_local = own_home.shape[1]
    audio_local = audio_out.shape[1]

    barrier = pltpu.get_barrier_semaphore()

    def greet(k, carry):
        peer = lax.rem(me + k, n)
        pl.semaphore_signal(barrier, inc=1, device_id=(group, peer), device_id_type=MESH)
        return carry

    lax.fori_loop(1, n, greet, 0)
    small = [
        pltpu.make_async_copy(source, target, small_sems.at[i])
        for i, (source, target) in enumerate(
            (
                (video_gate_far, video_gate),
                (audio_gate_far, audio_gate),
                (audio_valid_far, audio_valid),
                (branch_prompt_far, branch_prompt),
            )
        )
    ]
    for copy in small:
        copy.start()
    pl.semaphore_wait(barrier, n - 1)

    video_rows = pl.ds(pl.multiple_of(me * video_local, video_local), video_local)
    audio_rows = pl.ds(pl.multiple_of(me * audio_local, audio_local), audio_local)

    near, quarter = n // 2, n // 4
    my_half = me // near
    half_first = my_half * near
    place_in_half = me - half_first
    half_rows = pl.ds(pl.multiple_of(place_in_half * video_local, video_local), video_local)
    half_audio_rows = pl.ds(pl.multiple_of(place_in_half * audio_local, audio_local), audio_local)

    def is_inner(device):
        q = device // quarter
        return (q * (3 - q)) // 2

    inner = is_inner(me)
    outer_in_half = my_half * 3 * quarter

    def columns(head):
        return pl.ds(pl.multiple_of(head * HEAD, HEAD), HEAD)

    def video_place(device, slot):
        here = is_inner(device)
        high = device // near
        outside = (device - high * 2 * quarter) * video_outer + slot
        inside = 2 * quarter * video_outer + (device - quarter) * video_inner + slot
        item = outside + here * (inside - outside)
        return item // HV, lax.rem(item, HV)

    def cross_place(device, slot):
        item = lax.rem(device, near) * cross_count + slot
        return item // HV, lax.rem(item, HV)

    def audio_place(device, slot):
        here = is_inner(device)
        r = lax.rem(device, quarter)
        outside = r * audio_outer + slot
        inside = quarter * audio_outer + r * audio_inner + slot
        item = outside + here * (inside - outside)
        return item // HA, lax.rem(item, HA)

    def video_parts(peer, slot):
        branch, head = video_place(peer, slot)
        return (
            (
                video_qkv.at[branch, :, :, columns(head)],
                video_qkv_in.at[slot, :, video_rows],
                video_sems.at[slot],
            ),
        )

    def cross_q_parts(peer, slot):
        branch, head = cross_place(peer, slot)
        return (
            (
                video_q.at[branch, :, columns(head)],
                video_q_in.at[slot, half_rows],
                cross_sems.at[slot, 0],
            ),
        )

    def cross_kv_parts(peer, slot):
        branch, head = cross_place(peer, slot)
        return (
            (
                audio_kv.at[branch, :, :, columns(head)],
                audio_kv_in.at[slot, audio_rows],
                cross_sems.at[slot, 1],
            ),
        )

    def both_q_parts(peer, slot):
        branch, head = audio_place(peer, slot)
        return (
            (
                audio_qkv.at[branch, 0, :, columns(head)],
                both_q_in.at[slot, 0, audio_rows],
                both_sems.at[slot],
            ),
            (
                audio_q.at[branch, :, columns(head)],
                both_q_in.at[slot, 1, audio_rows],
                both_sems.at[slot],
            ),
        )

    def own_kv_parts(peer, slot):
        branch, head = audio_place(peer, slot)
        return (
            (
                audio_qkv.at[branch, 1:3, :, columns(head)],
                own_kv_in.at[slot, :, half_audio_rows],
                kv_sems.at[slot, 0],
            ),
        )

    def video_kv_parts(peer, slot):
        branch, head = audio_place(peer, slot)
        return (
            (
                video_kv.at[branch, :, :, columns(head)],
                video_kv_in.at[slot, half_rows],
                kv_sems.at[slot, 1],
            ),
        )

    def send(parts, slot, send_sem, first, span):
        place = lax.rem(me - first + n, n)
        member = 1 - jnp.minimum(place // span, 1)

        def to_peer(k, carry):
            step = k // 2 + lax.rem(k, 2) * (span // 2)
            peer = lax.rem(first + lax.rem(place + step, span), n)
            for source, target, sem in parts(peer, slot):
                pltpu.make_async_remote_copy(
                    src_ref=source,
                    dst_ref=target,
                    send_sem=send_sems.at[send_sem],
                    recv_sem=sem,
                    device_id=(group, peer),
                    device_id_type=MESH,
                ).start()
            return carry

        lax.fori_loop(member, span, to_peer, 0)

        @pl.when(member == 1)
        def _():
            for source, target, sem in parts(me, slot):
                pltpu.make_async_copy(source, target, sem).start()

    steps = video_inner + 1

    def cross_before(step):
        return step * cross_count // steps

    def send_step(step, carry):
        def send_cross(slot, inner_carry):
            send(cross_kv_parts, slot, 3, 0, n)
            send(cross_q_parts, slot, 2, half_first, near)
            return inner_carry

        lax.fori_loop(cross_before(step), cross_before(step + 1), send_cross, 0)
        @pl.when(step < video_outer)
        def _():
            send(video_parts, step, 0, 0, n)

        @pl.when((step >= video_outer) & (step < video_inner))
        def _():
            send(video_parts, step, 1, quarter, 2 * quarter)

        @pl.when(step < audio_inner)
        def _():
            send(both_q_parts, step, 4, 0, n)
            send(own_kv_parts, step, 6, half_first, near)
            send(video_kv_parts, step, 7, half_first, near)

        @pl.when((step >= audio_inner) & (step < audio_outer))
        def _():
            send(both_q_parts, step, 5, 3 * quarter, 2 * quarter)
            send(own_kv_parts, step, 8, outer_in_half, quarter)
            send(video_kv_parts, step, 9, outer_in_half, quarter)


        return carry

    lax.fori_loop(0, min(AHEAD, steps), send_step, 0)
    for copy in small:
        copy.wait()
    for branch in range(own_home.shape[0]):
        for first in range(0, own_home.shape[2], JOIN):
            here = slice(first, first + JOIN)
            video_gates[branch : branch + 1, here] = gate_of(branch_prompt, video_gate, branch, here)

    def mask(branch):
        positions = lax.broadcasted_iota(jnp.int32, (1, audio_kv_in.shape[1]), 1)
        return jnp.where(positions < audio_valid[branch], 0.0, -jnp.inf)

    def settle(ref, sem):
        pltpu.make_async_copy(ref, ref, sem).wait()

    def give_back(result, slot, out, branch, head, local, base, first, count, place):
        def to_peer(j, carry):
            peer = base + first + j
            source = result.at[slot, pl.ds(pl.multiple_of((first + j) * local, local), local)]
            target = out.at[branch, :, columns(head)]

            @pl.when(peer == me)
            def _():
                pltpu.make_async_copy(source, target, back_sems.at[place]).start()

            @pl.when(peer != me)
            def _():
                pltpu.make_async_remote_copy(
                    src_ref=source,
                    dst_ref=target,
                    send_sem=send_sems.at[10 + place],
                    recv_sem=back_sems.at[place],
                    device_id=(group, peer),
                    device_id_type=MESH,
                ).start()

            return carry

        lax.fori_loop(0, count, to_peer, 0)

    def part_kinds(source, slot, target):
        for first in range(0, target.shape[1], HEAD):
            here = slice(first, first + HEAD)
            target[:, here] = jnp.swapaxes(source[slot, here], 0, 1)

    def video_item(slot):
        branch, head = video_place(me, slot)
        settle(video_qkv_in.at[slot], video_sems.at[slot])
        block = video_block * video_local

        def rows(i, inner):
            here = pl.ds(pl.multiple_of(i * block, block), block)
            own, _ = attend(
                video_qkv_in[slot, 0, here], video_qkv_in[slot, 1], video_qkv_in[slot, 2], None
            )
            video_res[slot, here] = own.astype(jnp.bfloat16)
            give_back(
                video_res, slot, own_home, branch, head, video_local, 0, i * video_block,
                video_block, 0,
            )
            return inner

        lax.fori_loop(0, n // video_block, rows, 0)

    def cross_item(slot, carry):
        branch, head = cross_place(me, slot)
        settle(video_q_in.at[slot], cross_sems.at[slot, 0])
        settle(audio_kv_in.at[slot], cross_sems.at[slot, 1])
        part_kinds(audio_kv_in, slot, audio_pair)
        block = video_block * video_local

        def rows(i, inner):
            here = pl.ds(pl.multiple_of(i * block, block), block)
            cross, _ = attend(
                video_q_in[slot, here], audio_pair[0], audio_pair[1], mask(branch)
            )
            cross_res[slot, here] = cross.astype(jnp.bfloat16)
            give_back(
                cross_res, slot, cross_home, branch, head, video_local, half_first,
                i * video_block, video_block, 2,
            )
            return inner

        lax.fori_loop(0, near // video_block, rows, 0)
        return carry

    partner = (3 - me // quarter) * quarter + lax.rem(me, quarter)
    half_audio = near * audio_local
    chunks = n * audio_local // HEAD
    half_chunks = chunks // 2

    def half_mask(branch):
        positions = lax.broadcasted_iota(jnp.int32, (1, half_audio), 1) + my_half * half_audio
        return jnp.where(positions < audio_valid[branch], 0.0, -1e30)

    def to_partner(source, target, place, slot):
        pltpu.make_async_remote_copy(
            src_ref=source.at[slot],
            dst_ref=target.at[slot],
            send_sem=send_sems.at[13 + place],
            recv_sem=pair_sems.at[place, slot],
            device_id=(group, partner),
            device_id_type=MESH,
        ).start()

    def audio_item(slot):
        branch, head = audio_place(me, slot)
        settle(both_q_in.at[slot], both_sems.at[slot])
        settle(own_kv_in.at[slot], kv_sems.at[slot, 0])
        settle(video_kv_in.at[slot], kv_sems.at[slot, 1])
        part_kinds(video_kv_in, slot, video_pair)
        block = audio_block * audio_local
        per_block = block // HEAD

        def rows(i, inner):
            here = pl.ds(pl.multiple_of(i * block, block), block)
            for kind, (keys, bias) in enumerate(
                ((own_kv_in.at[slot], half_mask(branch)), (video_pair, None))
            ):
                part, level = attend(both_q_in[slot, kind, here], keys[0], keys[1], bias)
                part_res[slot, kind, here] = part
                for c in range(per_block):
                    column = jnp.broadcast_to(level[c * HEAD : (c + 1) * HEAD], (HEAD, HEAD))
                    level_res[slot, kind * chunks + i * per_block + c] = jnp.transpose(column)[0:1]
            return inner

        lax.fori_loop(0, n // audio_block, rows, 0)
        to_partner(level_res, level_in, 0, slot)

    def weighted(slot, chunk, gate):
        here = pl.ds(pl.multiple_of(chunk * HEAD, HEAD), HEAD)
        terms = []
        for kind in range(2):
            gap = level_in[slot, kind * chunks + chunk] - level_res[slot, kind * chunks + chunk]
            weight = jnp.transpose(jnp.broadcast_to(1.0 / (1.0 + jnp.exp(gap)), (HEAD, HEAD)))
            terms.append(weight * part_res[slot, kind, here])
        return terms[0] + gate * terms[1]

    def audio_share(slot):
        branch, head = audio_place(me, slot)
        settle(level_in.at[slot], pair_sems.at[0, slot])
        gate = gate_of(branch_prompt, audio_gate, branch, columns(head))
        for c in range(half_chunks):
            share_res[slot, c * HEAD : (c + 1) * HEAD] = weighted(
                slot, (1 - my_half) * half_chunks + c, gate
            ).astype(jnp.bfloat16)
        to_partner(share_res, share_in, 1, slot)

    def audio_final(slot):
        branch, head = audio_place(me, slot)
        settle(share_in.at[slot], pair_sems.at[1, slot])
        gate = gate_of(branch_prompt, audio_gate, branch, columns(head))
        for c in range(half_chunks):
            here = slice(c * HEAD, (c + 1) * HEAD)
            final_res[slot, here] = (
                weighted(slot, my_half * half_chunks + c, gate)
                + share_in[slot, here].astype(jnp.float32)
            ).astype(jnp.bfloat16)
        give_back(
            final_res, slot, audio_out, branch, head, audio_local, half_first, 0, near, 1
        )

    my_video = video_outer + inner * (video_inner - video_outer)
    my_audio = audio_outer + inner * (audio_inner - audio_outer)

    def work_step(step, carry):
        @pl.when(step + AHEAD < steps)
        def _():
            send_step(step + AHEAD, 0)

        @pl.when(step < my_audio)
        def _():
            audio_item(step)

        @pl.when(step < my_video)
        def _():
            video_item(step)

        @pl.when((step >= 1) & (step - 1 < my_audio))
        def _():
            audio_share(step - 1)

        lax.fori_loop(cross_before(step), cross_before(step + 1), cross_item, 0)

        @pl.when((step >= 2) & (step - 2 < my_audio))
        def _():
            audio_final(step - 2)

        return carry

    lax.fori_loop(0, steps, work_step, 0)

    @pl.when(my_audio == steps - 1)
    def _():
        audio_final(steps - 2)

    settle(own_home, back_sems.at[0])
    settle(cross_home, back_sems.at[2])
    settle(audio_out, back_sems.at[1])

    far_half = pl.ds(0, (near - 1) * video_local)
    far_video = pl.ds(0, (n - 1) * video_local)

    def few(count, local):
        return pl.ds(0, count * local)

    settle(video_qkv_in.at[0:video_outer, :, far_video], send_sems.at[0])
    settle(video_q_in.at[:, far_half], send_sems.at[2])
    settle(audio_kv_in.at[:, few(n - 1, audio_local)], send_sems.at[3])
    settle(both_q_in.at[0:audio_inner, :, few(n - 1, audio_local)], send_sems.at[4])
    settle(own_kv_in.at[0:audio_inner, :, few(near - 1, audio_local)], send_sems.at[6])
    settle(video_kv_in.at[0:audio_inner, far_half], send_sems.at[7])
    settle(cross_res.at[:, far_half], send_sems.at[12])

    for here in range(2):

        @pl.when(inner == here)
        def _():
            away = 1 - here
            more_video = pl.ds(video_outer, video_inner - video_outer)
            more_audio = pl.ds(audio_inner, audio_outer - audio_inner)
            videos = pl.ds(0, (video_outer, video_inner)[here])
            audios = pl.ds(0, (audio_outer, audio_inner)[here])
            settle(video_qkv_in.at[more_video, :, few(2 * quarter - here, video_local)], send_sems.at[1])
            settle(both_q_in.at[more_audio, :, few(2 * quarter - away, audio_local)], send_sems.at[5])
            settle(own_kv_in.at[more_audio, :, few(quarter - away, audio_local)], send_sems.at[8])
            settle(video_kv_in.at[more_audio, few(quarter - away, video_local)], send_sems.at[9])
            settle(video_res.at[videos, far_video], send_sems.at[10])
            settle(final_res.at[audios, few(near - 1, audio_local)], send_sems.at[11])
            settle(level_res.at[audios], send_sems.at[13])
            settle(share_res.at[audios], send_sems.at[14])


def kinds_first(source):
    return jnp.transpose(source, (0, 2, 1, 3))


def shares(total):
    return total // 4, total - total // 4


def on_device(
    n,
    video_qkv,
    video_cross_q,
    audio_kv_v,
    audio_qkv,
    audio_cross_q,
    video_kv_a,
    audio_valid,
    branch_prompt,
    video_gate,
    audio_gate,
):
    branches, video_local = video_cross_q.shape[:2]
    audio_local = audio_cross_q.shape[1]
    video_all, audio_all = video_local * n, audio_local * n
    near, quarter = n // 2, n // 4
    video_outer, video_inner = shares(branches * HV // near)
    cross_count = branches * HV // near
    audio_inner, audio_outer = shares(branches * HA // quarter)
    hbm = pl.BlockSpec(memory_space=pltpu.HBM)
    vmem = pl.BlockSpec(memory_space=pltpu.VMEM)
    half = jnp.bfloat16
    homes = pl.pallas_call(
        functools.partial(
            block_kernel,
            n,
            video_outer,
            video_inner,
            cross_count,
            audio_outer,
            audio_inner,
            min(4, near),
            min(8, n),
        ),
        out_shape=(
            jax.ShapeDtypeStruct(video_cross_q.shape, half),
            jax.ShapeDtypeStruct(video_cross_q.shape, half),
            jax.ShapeDtypeStruct(audio_cross_q.shape, half),
            jax.ShapeDtypeStruct((branches, video_gate.shape[1]), jnp.float32),
        ),
        in_specs=[hbm] * 10,
        out_specs=(vmem,) * 4,
        scratch_shapes=[
            pltpu.VMEM(video_gate.shape, jnp.float32),
            pltpu.VMEM(audio_gate.shape, jnp.float32),
            pltpu.SMEM(audio_valid.shape, jnp.int32),
            pltpu.SMEM(branch_prompt.shape, jnp.int32),
            pltpu.VMEM((video_inner, 3, video_all, HEAD), half),
            pltpu.VMEM((cross_count, near * video_local, HEAD), half),
            pltpu.VMEM((cross_count, audio_all, 2, HEAD), half),
            pltpu.VMEM((audio_outer, 2, audio_all, HEAD), half),
            pltpu.VMEM((audio_outer, 2, near * audio_local, HEAD), half),
            pltpu.VMEM((audio_outer, near * video_local, 2, HEAD), half),
            pltpu.VMEM((2, audio_all, HEAD), half),
            pltpu.VMEM((2, near * video_local, HEAD), half),
            pltpu.VMEM((video_inner, video_all, HEAD), half),
            pltpu.VMEM((cross_count, near * video_local, HEAD), half),
            pltpu.VMEM((audio_outer, 2, audio_all, HEAD), jnp.float32),
            pltpu.VMEM((audio_outer, 2 * audio_all // HEAD, 1, HEAD), jnp.float32),
            pltpu.VMEM((audio_outer, 2 * audio_all // HEAD, 1, HEAD), jnp.float32),
            pltpu.VMEM((audio_outer, near * audio_local, HEAD), half),
            pltpu.VMEM((audio_outer, near * audio_local, HEAD), half),
            pltpu.VMEM((audio_outer, near * audio_local, HEAD), half),
            pltpu.SemaphoreType.DMA((video_inner,)),
            pltpu.SemaphoreType.DMA((cross_count, 2)),
            pltpu.SemaphoreType.DMA((audio_outer,)),
            pltpu.SemaphoreType.DMA((audio_outer, 2)),
            pltpu.SemaphoreType.DMA((2, audio_outer)),
            pltpu.SemaphoreType.DMA((15,)),
            pltpu.SemaphoreType.DMA((3,)),
            pltpu.SemaphoreType.DMA((4,)),
        ],
        compiler_params=pltpu.CompilerParams(
            collective_id=0, has_side_effects=True, vmem_limit_bytes=48 * 2**20
        ),
    )(
        *(
            pltpu.with_memory_space_constraint(source, pltpu.HBM)
            for source in (
                kinds_first(video_qkv),
                video_cross_q,
                audio_kv_v,
                kinds_first(audio_qkv),
                audio_cross_q,
                video_kv_a,
                video_gate,
                audio_gate,
                audio_valid,
                branch_prompt,
            )
        )
    )
    return tuple(
        pl.pallas_call(
            join_kernel,
            out_shape=(
                jax.ShapeDtypeStruct(video_cross_q.shape, half),
                jax.ShapeDtypeStruct(audio_cross_q.shape, half),
            ),
            in_specs=[vmem] * 4,
            out_specs=(hbm, hbm),
            scratch_shapes=[
                pltpu.VMEM(video_cross_q.shape, half),
                pltpu.SemaphoreType.DMA((branches * video_cross_q.shape[2] // JOIN + 1,)),
            ],
            compiler_params=pltpu.CompilerParams(vmem_limit_bytes=4 * 2**20),
        )(*homes)
    )


def solution(mesh):
    placed = (
        P("groups", "seq", None, None),
        P("groups", "seq", None),
        P("groups", "seq", None, None),
        P("groups", "seq", None, None),
        P("groups", "seq", None),
        P("groups", "seq", None, None),
        P("groups"),
        P("groups"),
        P(),
        P(),
    )
    return jax.shard_map(
        functools.partial(on_device, mesh.shape["seq"]),
        mesh=mesh,
        in_specs=placed,
        out_specs=(P("groups", "seq", None), P("groups", "seq", None)),
        check_vma=False,
    )
```

```python
import functools

import jax
import jax.numpy as jnp
from jax import lax
from jax.experimental import pallas as pl
from jax.experimental.pallas import tpu as pltpu
from jax.sharding import PartitionSpec as P

HV = 32
HA = 16
HEAD = 128
PROMPTS = 4
MESH = pl.DeviceIdType.MESH
AHEAD = 2
JOIN = 1024


def attend(queries, key_rows, value_rows, bias):
    scores = lax.dot_general(
        queries, key_rows, (((1,), (1,)), ((), ())), preferred_element_type=jnp.float32
    ) * (HEAD**-0.5)
    if bias is not None:
        scores = scores + bias
    row_max = jnp.max(scores, axis=1, keepdims=True)
    weights = jnp.exp(scores - row_max)
    total = jnp.sum(weights, axis=1, keepdims=True)
    result = jnp.dot(
        weights.astype(jnp.bfloat16), value_rows, preferred_element_type=jnp.float32
    )
    return result / total, row_max + jnp.log(total)


def gate_of(branch_prompt, gates, branch, here):
    return sum(
        (branch_prompt[branch] == p).astype(jnp.int32).astype(jnp.float32)
        * gates[p : p + 1, here]
        for p in range(PROMPTS)
    )


def join_kernel(
    own_home, cross_home, audio_home, video_gates, video_out, audio_out, joined, sems
):
    width = JOIN
    branches, parts = own_home.shape[0], own_home.shape[2] // width
    audio = pltpu.make_async_copy(audio_home, audio_out, sems.at[branches * parts])
    audio.start()
    for branch in range(branches):
        for i in range(parts):
            here = slice(i * width, (i + 1) * width)
            joined[branch, :, here] = (
                own_home[branch, :, here].astype(jnp.float32)
                + video_gates[branch : branch + 1, here]
                * cross_home[branch, :, here].astype(jnp.float32)
            ).astype(jnp.bfloat16)
            pltpu.make_async_copy(
                joined.at[branch, :, here], video_out.at[branch, :, here], sems.at[branch * parts + i]
            ).start()
    for branch in range(branches):
        for i in range(parts):
            here = slice(i * width, (i + 1) * width)
            pltpu.make_async_copy(
                joined.at[branch, :, here], video_out.at[branch, :, here], sems.at[branch * parts + i]
            ).wait()
    audio.wait()


def block_kernel(
    n,
    video_outer,
    video_inner,
    cross_count,
    audio_outer,
    audio_inner,
    video_block,
    audio_block,
    video_qkv,
    video_q,
    audio_kv,
    audio_qkv,
    audio_q,
    video_kv,
    video_gate_far,
    audio_gate_far,
    audio_valid_far,
    branch_prompt_far,
    own_home,
    cross_home,
    audio_out,
    video_gates,
    video_gate,
    audio_gate,
    audio_valid,
    branch_prompt,
    video_qkv_in,
    video_q_in,
    audio_kv_in,
    both_q_in,
    own_kv_in,
    video_kv_in,
    audio_pair,
    video_pair,
    video_res,
    cross_res,
    part_res,
    level_res,
    level_in,
    share_res,
    share_in,
    final_res,
    video_sems,
    cross_sems,
    both_sems,
    kv_sems,
    pair_sems,
    send_sems,
    back_sems,
    small_sems,
):
    me = lax.axis_index("seq")
    group = lax.axis_index("groups")
    video_local = own_home.shape[1]
    audio_local = audio_out.shape[1]

    barrier = pltpu.get_barrier_semaphore()

    def greet(k, carry):
        peer = lax.rem(me + k, n)
        pl.semaphore_signal(barrier, inc=1, device_id=(group, peer), device_id_type=MESH)
        return carry

    lax.fori_loop(1, n, greet, 0)
    small = [
        pltpu.make_async_copy(source, target, small_sems.at[i])
        for i, (source, target) in enumerate(
            (
                (video_gate_far, video_gate),
                (audio_gate_far, audio_gate),
                (audio_valid_far, audio_valid),
                (branch_prompt_far, branch_prompt),
            )
        )
    ]
    for copy in small:
        copy.start()
    pl.semaphore_wait(barrier, n - 1)

    video_rows = pl.ds(pl.multiple_of(me * video_local, video_local), video_local)
    audio_rows = pl.ds(pl.multiple_of(me * audio_local, audio_local), audio_local)

    near, quarter = n // 2, n // 4
    my_half = me // near
    half_first = my_half * near
    place_in_half = me - half_first
    half_rows = pl.ds(pl.multiple_of(place_in_half * video_local, video_local), video_local)
    half_audio_rows = pl.ds(pl.multiple_of(place_in_half * audio_local, audio_local), audio_local)

    def is_inner(device):
        q = device // quarter
        return (q * (3 - q)) // 2

    inner = is_inner(me)
    outer_in_half = my_half * 3 * quarter

    def columns(head):
        return pl.ds(pl.multiple_of(head * HEAD, HEAD), HEAD)

    def video_place(device, slot):
        here = is_inner(device)
        high = device // near
        outside = (device - high * 2 * quarter) * video_outer + slot
        inside = 2 * quarter * video_outer + (device - quarter) * video_inner + slot
        item = outside + here * (inside - outside)
        return item // HV, lax.rem(item, HV)

    def cross_place(device, slot):
        item = lax.rem(device, near) * cross_count + slot
        return item // HV, lax.rem(item, HV)

    def audio_place(device, slot):
        here = is_inner(device)
        r = lax.rem(device, quarter)
        outside = r * audio_outer + slot
        inside = quarter * audio_outer + r * audio_inner + slot
        item = outside + here * (inside - outside)
        return item // HA, lax.rem(item, HA)

    def video_parts(peer, slot):
        branch, head = video_place(peer, slot)
        return (
            (
                video_qkv.at[branch, :, :, columns(head)],
                video_qkv_in.at[slot, :, video_rows],
                video_sems.at[slot],
            ),
        )

    def cross_q_parts(peer, slot):
        branch, head = cross_place(peer, slot)
        return (
            (
                video_q.at[branch, :, columns(head)],
                video_q_in.at[slot, half_rows],
                cross_sems.at[slot, 0],
            ),
        )

    def cross_kv_parts(peer, slot):
        branch, head = cross_place(peer, slot)
        return (
            (
                audio_kv.at[branch, :, :, columns(head)],
                audio_kv_in.at[slot, audio_rows],
                cross_sems.at[slot, 1],
            ),
        )

    def both_q_parts(peer, slot):
        branch, head = audio_place(peer, slot)
        return (
            (
                audio_qkv.at[branch, 0, :, columns(head)],
                both_q_in.at[slot, 0, audio_rows],
                both_sems.at[slot],
            ),
            (
                audio_q.at[branch, :, columns(head)],
                both_q_in.at[slot, 1, audio_rows],
                both_sems.at[slot],
            ),
        )

    def own_kv_parts(peer, slot):
        branch, head = audio_place(peer, slot)
        return (
            (
                audio_qkv.at[branch, 1:3, :, columns(head)],
                own_kv_in.at[slot, :, half_audio_rows],
                kv_sems.at[slot, 0],
            ),
        )

    def video_kv_parts(peer, slot):
        branch, head = audio_place(peer, slot)
        return (
            (
                video_kv.at[branch, :, :, columns(head)],
                video_kv_in.at[slot, half_rows],
                kv_sems.at[slot, 1],
            ),
        )

    def send(parts, slot, send_sem, first, span):
        place = lax.rem(me - first + n, n)
        member = 1 - jnp.minimum(place // span, 1)

        def to_peer(k, carry):
            step = k // 2 + lax.rem(k, 2) * (span // 2)
            peer = lax.rem(first + lax.rem(place + step, span), n)
            for source, target, sem in parts(peer, slot):
                pltpu.make_async_remote_copy(
                    src_ref=source,
                    dst_ref=target,
                    send_sem=send_sems.at[send_sem],
                    recv_sem=sem,
                    device_id=(group, peer),
                    device_id_type=MESH,
                ).start()
            return carry

        lax.fori_loop(member, span, to_peer, 0)

        @pl.when(member == 1)
        def _():
            for source, target, sem in parts(me, slot):
                pltpu.make_async_copy(source, target, sem).start()

    steps = video_inner + 1

    def cross_before(step):
        return (step * cross_count + steps // 2) // steps

    def audio_before(step):
        return jnp.minimum(step + jnp.minimum(step // 2, 1), audio_outer)

    def send_step(step, carry):
        def send_cross(slot, inner_carry):
            send(cross_kv_parts, slot, 3, 0, n)
            send(cross_q_parts, slot, 2, half_first, near)
            return inner_carry

        lax.fori_loop(cross_before(step), cross_before(step + 1), send_cross, 0)
        @pl.when(step < video_outer)
        def _():
            send(video_parts, step, 0, 0, n)

        @pl.when((step >= video_outer) & (step < video_inner))
        def _():
            send(video_parts, step, 1, quarter, 2 * quarter)

        def send_audio(slot, inner_carry):
            @pl.when(slot < audio_inner)
            def _():
                send(both_q_parts, slot, 4, 0, n)
                send(own_kv_parts, slot, 6, half_first, near)
                send(video_kv_parts, slot, 7, half_first, near)

            @pl.when(slot >= audio_inner)
            def _():
                send(both_q_parts, slot, 5, 3 * quarter, 2 * quarter)
                send(own_kv_parts, slot, 8, outer_in_half, quarter)
                send(video_kv_parts, slot, 9, outer_in_half, quarter)

            return inner_carry

        lax.fori_loop(audio_before(step), audio_before(step + 1), send_audio, 0)


        return carry

    lax.fori_loop(0, min(AHEAD, steps), send_step, 0)
    for copy in small:
        copy.wait()
    for branch in range(own_home.shape[0]):
        for first in range(0, own_home.shape[2], JOIN):
            here = slice(first, first + JOIN)
            video_gates[branch : branch + 1, here] = gate_of(branch_prompt, video_gate, branch, here)

    def mask(branch):
        positions = lax.broadcasted_iota(jnp.int32, (1, audio_kv_in.shape[1]), 1)
        return jnp.where(positions < audio_valid[branch], 0.0, -jnp.inf)

    def settle(ref, sem):
        pltpu.make_async_copy(ref, ref, sem).wait()

    def give_back(result, slot, out, branch, head, local, base, first, count, place):
        def to_peer(j, carry):
            peer = base + first + j
            source = result.at[slot, pl.ds(pl.multiple_of((first + j) * local, local), local)]
            target = out.at[branch, :, columns(head)]

            @pl.when(peer == me)
            def _():
                pltpu.make_async_copy(source, target, back_sems.at[place]).start()

            @pl.when(peer != me)
            def _():
                pltpu.make_async_remote_copy(
                    src_ref=source,
                    dst_ref=target,
                    send_sem=send_sems.at[10 + place],
                    recv_sem=back_sems.at[place],
                    device_id=(group, peer),
                    device_id_type=MESH,
                ).start()

            return carry

        lax.fori_loop(0, count, to_peer, 0)

    def part_kinds(source, slot, target):
        for first in range(0, target.shape[1], HEAD):
            here = slice(first, first + HEAD)
            target[:, here] = jnp.swapaxes(source[slot, here], 0, 1)

    def video_item(slot):
        branch, head = video_place(me, slot)
        settle(video_qkv_in.at[slot], video_sems.at[slot])
        block = video_block * video_local

        def rows(i, inner):
            here = pl.ds(pl.multiple_of(i * block, block), block)
            own, _ = attend(
                video_qkv_in[slot, 0, here], video_qkv_in[slot, 1], video_qkv_in[slot, 2], None
            )
            video_res[slot, here] = own.astype(jnp.bfloat16)
            give_back(
                video_res, slot, own_home, branch, head, video_local, 0, i * video_block,
                video_block, 0,
            )
            return inner

        lax.fori_loop(0, n // video_block, rows, 0)

    def cross_item(slot, carry):
        branch, head = cross_place(me, slot)
        settle(video_q_in.at[slot], cross_sems.at[slot, 0])
        settle(audio_kv_in.at[slot], cross_sems.at[slot, 1])
        part_kinds(audio_kv_in, slot, audio_pair)
        block = video_block * video_local

        def rows(i, inner):
            here = pl.ds(pl.multiple_of(i * block, block), block)
            cross, _ = attend(
                video_q_in[slot, here], audio_pair[0], audio_pair[1], mask(branch)
            )
            cross_res[slot, here] = cross.astype(jnp.bfloat16)
            give_back(
                cross_res, slot, cross_home, branch, head, video_local, half_first,
                i * video_block, video_block, 2,
            )
            return inner

        lax.fori_loop(0, near // video_block, rows, 0)
        return carry

    partner = (3 - me // quarter) * quarter + lax.rem(me, quarter)
    half_audio = near * audio_local
    chunks = n * audio_local // HEAD
    half_chunks = chunks // 2

    def half_mask(branch):
        positions = lax.broadcasted_iota(jnp.int32, (1, half_audio), 1) + my_half * half_audio
        return jnp.where(positions < audio_valid[branch], 0.0, -1e30)

    def to_partner(source, target, place, slot):
        pltpu.make_async_remote_copy(
            src_ref=source.at[slot],
            dst_ref=target.at[slot],
            send_sem=send_sems.at[13 + place],
            recv_sem=pair_sems.at[place, slot],
            device_id=(group, partner),
            device_id_type=MESH,
        ).start()

    def audio_item(slot):
        branch, head = audio_place(me, slot)
        settle(both_q_in.at[slot], both_sems.at[slot])
        settle(own_kv_in.at[slot], kv_sems.at[slot, 0])
        settle(video_kv_in.at[slot], kv_sems.at[slot, 1])
        part_kinds(video_kv_in, slot, video_pair)
        block = audio_block * audio_local
        per_block = block // HEAD

        def rows(i, inner):
            here = pl.ds(pl.multiple_of(i * block, block), block)
            for kind, (keys, bias) in enumerate(
                ((own_kv_in.at[slot], half_mask(branch)), (video_pair, None))
            ):
                part, level = attend(both_q_in[slot, kind, here], keys[0], keys[1], bias)
                part_res[slot, kind, here] = part
                for c in range(per_block):
                    column = jnp.broadcast_to(level[c * HEAD : (c + 1) * HEAD], (HEAD, HEAD))
                    level_res[slot, kind * chunks + i * per_block + c] = jnp.transpose(column)[0:1]
            return inner

        lax.fori_loop(0, n // audio_block, rows, 0)
        to_partner(level_res, level_in, 0, slot)

    def weighted(slot, chunk, gate):
        here = pl.ds(pl.multiple_of(chunk * HEAD, HEAD), HEAD)
        terms = []
        for kind in range(2):
            gap = level_in[slot, kind * chunks + chunk] - level_res[slot, kind * chunks + chunk]
            weight = jnp.transpose(jnp.broadcast_to(1.0 / (1.0 + jnp.exp(gap)), (HEAD, HEAD)))
            terms.append(weight * part_res[slot, kind, here])
        return terms[0] + gate * terms[1]

    def audio_share(slot):
        branch, head = audio_place(me, slot)
        settle(level_in.at[slot], pair_sems.at[0, slot])
        gate = gate_of(branch_prompt, audio_gate, branch, columns(head))
        for c in range(half_chunks):
            share_res[slot, c * HEAD : (c + 1) * HEAD] = weighted(
                slot, (1 - my_half) * half_chunks + c, gate
            ).astype(jnp.bfloat16)
        to_partner(share_res, share_in, 1, slot)

    def audio_final(slot):
        branch, head = audio_place(me, slot)
        settle(share_in.at[slot], pair_sems.at[1, slot])
        gate = gate_of(branch_prompt, audio_gate, branch, columns(head))
        for c in range(half_chunks):
            here = slice(c * HEAD, (c + 1) * HEAD)
            final_res[slot, here] = (
                weighted(slot, my_half * half_chunks + c, gate)
                + share_in[slot, here].astype(jnp.float32)
            ).astype(jnp.bfloat16)
        give_back(
            final_res, slot, audio_out, branch, head, audio_local, half_first, 0, near, 1
        )

    my_video = video_outer + inner * (video_inner - video_outer)
    my_audio = audio_outer + inner * (audio_inner - audio_outer)

    def audio_steps(step, work):
        def one(slot, carry):
            work(slot)
            return carry

        first, last = (audio_before(jnp.maximum(edge, 0)) for edge in (step, step + 1))
        lax.fori_loop(jnp.minimum(first, my_audio), jnp.minimum(last, my_audio), one, 0)

    def work_step(step, carry):
        @pl.when(step + AHEAD < steps)
        def _():
            send_step(step + AHEAD, 0)

        audio_steps(step, audio_item)

        @pl.when(step < my_video)
        def _():
            video_item(step)

        audio_steps(step - 1, audio_share)

        lax.fori_loop(cross_before(step), cross_before(step + 1), cross_item, 0)

        audio_steps(step - 2, audio_final)

        return carry

    lax.fori_loop(0, steps, work_step, 0)

    settle(own_home, back_sems.at[0])
    settle(cross_home, back_sems.at[2])
    settle(audio_out, back_sems.at[1])

    far_half = pl.ds(0, (near - 1) * video_local)
    far_video = pl.ds(0, (n - 1) * video_local)

    def few(count, local):
        return pl.ds(0, count * local)

    settle(video_qkv_in.at[0:video_outer, :, far_video], send_sems.at[0])
    settle(video_q_in.at[:, far_half], send_sems.at[2])
    settle(audio_kv_in.at[:, few(n - 1, audio_local)], send_sems.at[3])
    settle(both_q_in.at[0:audio_inner, :, few(n - 1, audio_local)], send_sems.at[4])
    settle(own_kv_in.at[0:audio_inner, :, few(near - 1, audio_local)], send_sems.at[6])
    settle(video_kv_in.at[0:audio_inner, far_half], send_sems.at[7])
    settle(cross_res.at[:, far_half], send_sems.at[12])

    for here in range(2):

        @pl.when(inner == here)
        def _():
            away = 1 - here
            more_video = pl.ds(video_outer, video_inner - video_outer)
            more_audio = pl.ds(audio_inner, audio_outer - audio_inner)
            videos = pl.ds(0, (video_outer, video_inner)[here])
            audios = pl.ds(0, (audio_outer, audio_inner)[here])
            settle(video_qkv_in.at[more_video, :, few(2 * quarter - here, video_local)], send_sems.at[1])
            settle(both_q_in.at[more_audio, :, few(2 * quarter - away, audio_local)], send_sems.at[5])
            settle(own_kv_in.at[more_audio, :, few(quarter - away, audio_local)], send_sems.at[8])
            settle(video_kv_in.at[more_audio, few(quarter - away, video_local)], send_sems.at[9])
            settle(video_res.at[videos, far_video], send_sems.at[10])
            settle(final_res.at[audios, few(near - 1, audio_local)], send_sems.at[11])
            settle(level_res.at[audios], send_sems.at[13])
            settle(share_res.at[audios], send_sems.at[14])


def kinds_first(source):
    return jnp.transpose(source, (0, 2, 1, 3))


def shares(total):
    return total // 4, total - total // 4


def on_device(
    n,
    video_qkv,
    video_cross_q,
    audio_kv_v,
    audio_qkv,
    audio_cross_q,
    video_kv_a,
    audio_valid,
    branch_prompt,
    video_gate,
    audio_gate,
):
    branches, video_local = video_cross_q.shape[:2]
    audio_local = audio_cross_q.shape[1]
    video_all, audio_all = video_local * n, audio_local * n
    near, quarter = n // 2, n // 4
    video_outer, video_inner = shares(branches * HV // near)
    cross_count = branches * HV // near
    audio_inner, audio_outer = shares(branches * HA // quarter)
    hbm = pl.BlockSpec(memory_space=pltpu.HBM)
    vmem = pl.BlockSpec(memory_space=pltpu.VMEM)
    half = jnp.bfloat16
    homes = pl.pallas_call(
        functools.partial(
            block_kernel,
            n,
            video_outer,
            video_inner,
            cross_count,
            audio_outer,
            audio_inner,
            min(4, near),
            min(8, n),
        ),
        out_shape=(
            jax.ShapeDtypeStruct(video_cross_q.shape, half),
            jax.ShapeDtypeStruct(video_cross_q.shape, half),
            jax.ShapeDtypeStruct(audio_cross_q.shape, half),
            jax.ShapeDtypeStruct((branches, video_gate.shape[1]), jnp.float32),
        ),
        in_specs=[hbm] * 10,
        out_specs=(vmem,) * 4,
        scratch_shapes=[
            pltpu.VMEM(video_gate.shape, jnp.float32),
            pltpu.VMEM(audio_gate.shape, jnp.float32),
            pltpu.SMEM(audio_valid.shape, jnp.int32),
            pltpu.SMEM(branch_prompt.shape, jnp.int32),
            pltpu.VMEM((video_inner, 3, video_all, HEAD), half),
            pltpu.VMEM((cross_count, near * video_local, HEAD), half),
            pltpu.VMEM((cross_count, audio_all, 2, HEAD), half),
            pltpu.VMEM((audio_outer, 2, audio_all, HEAD), half),
            pltpu.VMEM((audio_outer, 2, near * audio_local, HEAD), half),
            pltpu.VMEM((audio_outer, near * video_local, 2, HEAD), half),
            pltpu.VMEM((2, audio_all, HEAD), half),
            pltpu.VMEM((2, near * video_local, HEAD), half),
            pltpu.VMEM((video_inner, video_all, HEAD), half),
            pltpu.VMEM((cross_count, near * video_local, HEAD), half),
            pltpu.VMEM((audio_outer, 2, audio_all, HEAD), jnp.float32),
            pltpu.VMEM((audio_outer, 2 * audio_all // HEAD, 1, HEAD), jnp.float32),
            pltpu.VMEM((audio_outer, 2 * audio_all // HEAD, 1, HEAD), jnp.float32),
            pltpu.VMEM((audio_outer, near * audio_local, HEAD), half),
            pltpu.VMEM((audio_outer, near * audio_local, HEAD), half),
            pltpu.VMEM((audio_outer, near * audio_local, HEAD), half),
            pltpu.SemaphoreType.DMA((video_inner,)),
            pltpu.SemaphoreType.DMA((cross_count, 2)),
            pltpu.SemaphoreType.DMA((audio_outer,)),
            pltpu.SemaphoreType.DMA((audio_outer, 2)),
            pltpu.SemaphoreType.DMA((2, audio_outer)),
            pltpu.SemaphoreType.DMA((15,)),
            pltpu.SemaphoreType.DMA((3,)),
            pltpu.SemaphoreType.DMA((4,)),
        ],
        compiler_params=pltpu.CompilerParams(
            collective_id=0, has_side_effects=True, vmem_limit_bytes=48 * 2**20
        ),
    )(
        *(
            pltpu.with_memory_space_constraint(source, pltpu.HBM)
            for source in (
                kinds_first(video_qkv),
                video_cross_q,
                audio_kv_v,
                kinds_first(audio_qkv),
                audio_cross_q,
                video_kv_a,
                video_gate,
                audio_gate,
                audio_valid,
                branch_prompt,
            )
        )
    )
    return tuple(
        pl.pallas_call(
            join_kernel,
            out_shape=(
                jax.ShapeDtypeStruct(video_cross_q.shape, half),
                jax.ShapeDtypeStruct(audio_cross_q.shape, half),
            ),
            in_specs=[vmem] * 4,
            out_specs=(hbm, hbm),
            scratch_shapes=[
                pltpu.VMEM(video_cross_q.shape, half),
                pltpu.SemaphoreType.DMA((branches * video_cross_q.shape[2] // JOIN + 1,)),
            ],
            compiler_params=pltpu.CompilerParams(vmem_limit_bytes=4 * 2**20),
        )(*homes)
    )


def solution(mesh):
    placed = (
        P("groups", "seq", None, None),
        P("groups", "seq", None),
        P("groups", "seq", None, None),
        P("groups", "seq", None, None),
        P("groups", "seq", None),
        P("groups", "seq", None, None),
        P("groups"),
        P("groups"),
        P(),
        P(),
    )
    return jax.shard_map(
        functools.partial(on_device, mesh.shape["seq"]),
        mesh=mesh,
        in_specs=placed,
        out_specs=(P("groups", "seq", None), P("groups", "seq", None)),
        check_vma=False,
    )
```

```python
import functools

import jax
import jax.numpy as jnp
from jax import lax
from jax.experimental import pallas as pl
from jax.experimental.pallas import tpu as pltpu
from jax.sharding import PartitionSpec as P

HV = 32
HA = 16
HEAD = 128
PROMPTS = 4
MESH = pl.DeviceIdType.MESH
AHEAD = 2
JOIN = 1024


def attend(queries, key_rows, value_rows, bias):
    scores = lax.dot_general(
        queries, key_rows, (((1,), (1,)), ((), ())), preferred_element_type=jnp.float32
    ) * (HEAD**-0.5)
    if bias is not None:
        scores = scores + bias
    row_max = jnp.max(scores, axis=1, keepdims=True)
    weights = jnp.exp(scores - row_max)
    total = jnp.sum(weights, axis=1, keepdims=True)
    result = jnp.dot(
        weights.astype(jnp.bfloat16), value_rows, preferred_element_type=jnp.float32
    )
    return result / total, row_max + jnp.log(total)


def gate_of(branch_prompt, gates, branch, here):
    return sum(
        (branch_prompt[branch] == p).astype(jnp.int32).astype(jnp.float32)
        * gates[p : p + 1, here]
        for p in range(PROMPTS)
    )


def join_kernel(
    own_home, cross_home, audio_home, video_gates, video_out, audio_out, joined, sems
):
    width = JOIN
    branches, parts = own_home.shape[0], own_home.shape[2] // width
    audio = pltpu.make_async_copy(audio_home, audio_out, sems.at[branches * parts])
    audio.start()
    for branch in range(branches):
        for i in range(parts):
            here = slice(i * width, (i + 1) * width)
            joined[branch, :, here] = (
                own_home[branch, :, here].astype(jnp.float32)
                + video_gates[branch : branch + 1, here]
                * cross_home[branch, :, here].astype(jnp.float32)
            ).astype(jnp.bfloat16)
            pltpu.make_async_copy(
                joined.at[branch, :, here], video_out.at[branch, :, here], sems.at[branch * parts + i]
            ).start()
    for branch in range(branches):
        for i in range(parts):
            here = slice(i * width, (i + 1) * width)
            pltpu.make_async_copy(
                joined.at[branch, :, here], video_out.at[branch, :, here], sems.at[branch * parts + i]
            ).wait()
    audio.wait()


def block_kernel(
    n,
    video_outer,
    video_inner,
    cross_count,
    audio_outer,
    audio_inner,
    video_block,
    audio_block,
    video_qkv,
    video_q,
    audio_kv,
    audio_qkv,
    audio_q,
    video_kv,
    video_gate_far,
    audio_gate_far,
    audio_valid_far,
    branch_prompt_far,
    own_home,
    cross_home,
    audio_out,
    video_gates,
    video_gate,
    audio_gate,
    audio_valid,
    branch_prompt,
    video_qkv_in,
    video_q_in,
    audio_kv_in,
    both_q_in,
    own_kv_in,
    video_kv_in,
    audio_pair,
    video_pair,
    video_res,
    cross_res,
    part_res,
    level_res,
    level_in,
    share_res,
    share_in,
    final_res,
    video_sems,
    cross_sems,
    both_sems,
    kv_sems,
    pair_sems,
    send_sems,
    back_sems,
    small_sems,
):
    me = lax.axis_index("seq")
    group = lax.axis_index("groups")
    video_local = own_home.shape[1]
    audio_local = audio_out.shape[1]

    barrier = pltpu.get_barrier_semaphore()

    def greet(k, carry):
        peer = lax.rem(me + k, n)
        pl.semaphore_signal(barrier, inc=1, device_id=(group, peer), device_id_type=MESH)
        return carry

    lax.fori_loop(1, n, greet, 0)
    small = [
        pltpu.make_async_copy(source, target, small_sems.at[i])
        for i, (source, target) in enumerate(
            (
                (video_gate_far, video_gate),
                (audio_gate_far, audio_gate),
                (audio_valid_far, audio_valid),
                (branch_prompt_far, branch_prompt),
            )
        )
    ]
    for copy in small:
        copy.start()
    pl.semaphore_wait(barrier, n - 1)

    video_rows = pl.ds(pl.multiple_of(me * video_local, video_local), video_local)
    audio_rows = pl.ds(pl.multiple_of(me * audio_local, audio_local), audio_local)

    near, quarter = n // 2, n // 4
    my_half = me // near
    half_first = my_half * near
    place_in_half = me - half_first
    half_rows = pl.ds(pl.multiple_of(place_in_half * video_local, video_local), video_local)
    half_audio_rows = pl.ds(pl.multiple_of(place_in_half * audio_local, audio_local), audio_local)

    def is_inner(device):
        q = device // quarter
        return (q * (3 - q)) // 2

    inner = is_inner(me)
    outer_in_half = my_half * 3 * quarter

    def columns(head):
        return pl.ds(pl.multiple_of(head * HEAD, HEAD), HEAD)

    def video_place(device, slot):
        here = is_inner(device)
        high = device // near
        outside = (device - high * 2 * quarter) * video_outer + slot
        inside = 2 * quarter * video_outer + (device - quarter) * video_inner + slot
        item = outside + here * (inside - outside)
        return item // HV, lax.rem(item, HV)

    def cross_place(device, slot):
        item = lax.rem(device, near) * cross_count + slot
        return item // HV, lax.rem(item, HV)

    def audio_place(device, slot):
        here = is_inner(device)
        r = lax.rem(device, quarter)
        outside = r * audio_outer + slot
        inside = quarter * audio_outer + r * audio_inner + slot
        item = outside + here * (inside - outside)
        return item // HA, lax.rem(item, HA)

    def video_parts(peer, slot):
        branch, head = video_place(peer, slot)
        return (
            (
                video_qkv.at[branch, :, :, columns(head)],
                video_qkv_in.at[slot, :, video_rows],
                video_sems.at[slot],
            ),
        )

    def cross_q_parts(peer, slot):
        branch, head = cross_place(peer, slot)
        return (
            (
                video_q.at[branch, :, columns(head)],
                video_q_in.at[slot, half_rows],
                cross_sems.at[slot, 0],
            ),
        )

    def cross_kv_parts(peer, slot):
        branch, head = cross_place(peer, slot)
        return (
            (
                audio_kv.at[branch, :, :, columns(head)],
                audio_kv_in.at[slot, audio_rows],
                cross_sems.at[slot, 1],
            ),
        )

    def both_q_parts(peer, slot):
        branch, head = audio_place(peer, slot)
        return (
            (
                audio_qkv.at[branch, 0, :, columns(head)],
                both_q_in.at[slot, 0, audio_rows],
                both_sems.at[slot],
            ),
            (
                audio_q.at[branch, :, columns(head)],
                both_q_in.at[slot, 1, audio_rows],
                both_sems.at[slot],
            ),
        )

    def own_kv_parts(peer, slot):
        branch, head = audio_place(peer, slot)
        return (
            (
                audio_qkv.at[branch, 1:3, :, columns(head)],
                own_kv_in.at[slot, :, half_audio_rows],
                kv_sems.at[slot, 0],
            ),
        )

    def video_kv_parts(peer, slot):
        branch, head = audio_place(peer, slot)
        return (
            (
                video_kv.at[branch, :, :, columns(head)],
                video_kv_in.at[slot, half_rows],
                kv_sems.at[slot, 1],
            ),
        )

    def send(parts, slot, send_sem, first, span):
        place = lax.rem(me - first + n, n)
        member = 1 - jnp.minimum(place // span, 1)

        def to_peer(k, carry):
            step = k // 2 + lax.rem(k, 2) * (span // 2)
            peer = lax.rem(first + lax.rem(place + step, span), n)
            for source, target, sem in parts(peer, slot):
                pltpu.make_async_remote_copy(
                    src_ref=source,
                    dst_ref=target,
                    send_sem=send_sems.at[send_sem],
                    recv_sem=sem,
                    device_id=(group, peer),
                    device_id_type=MESH,
                ).start()
            return carry

        lax.fori_loop(member, span, to_peer, 0)

        @pl.when(member == 1)
        def _():
            for source, target, sem in parts(me, slot):
                pltpu.make_async_copy(source, target, sem).start()

    steps = video_inner + 1

    def cross_before(step):
        return (step * cross_count + steps // 2) // steps

    def audio_before(step):
        return jnp.minimum(step + jnp.minimum(step // 2, 1), audio_outer)

    def send_step(step, carry):
        def send_cross(slot, inner_carry):
            send(cross_kv_parts, slot, 3, 0, n)
            send(cross_q_parts, slot, 2, half_first, near)
            return inner_carry

        lax.fori_loop(cross_before(step), cross_before(step + 1), send_cross, 0)
        @pl.when(step < video_outer)
        def _():
            send(video_parts, step, 0, 0, n)

        @pl.when((step >= video_outer) & (step < video_inner))
        def _():
            send(video_parts, step, 1, quarter, 2 * quarter)

        def send_audio(slot, inner_carry):
            @pl.when(slot < audio_inner)
            def _():
                send(both_q_parts, slot, 4, 0, n)
                send(own_kv_parts, slot, 6, half_first, near)
                send(video_kv_parts, slot, 7, half_first, near)

            @pl.when(slot >= audio_inner)
            def _():
                send(both_q_parts, slot, 5, 3 * quarter, 2 * quarter)
                send(own_kv_parts, slot, 8, outer_in_half, quarter)
                send(video_kv_parts, slot, 9, outer_in_half, quarter)

            return inner_carry

        lax.fori_loop(audio_before(step), audio_before(step + 1), send_audio, 0)


        return carry

    lax.fori_loop(0, min(AHEAD, steps), send_step, 0)
    for copy in small:
        copy.wait()
    for branch in range(own_home.shape[0]):
        for first in range(0, own_home.shape[2], JOIN):
            here = slice(first, first + JOIN)
            video_gates[branch : branch + 1, here] = gate_of(branch_prompt, video_gate, branch, here)

    def mask(branch):
        positions = lax.broadcasted_iota(jnp.int32, (1, audio_kv_in.shape[1]), 1)
        return jnp.where(positions < audio_valid[branch], 0.0, -jnp.inf)

    def settle(ref, sem):
        pltpu.make_async_copy(ref, ref, sem).wait()

    def give_back(result, slot, out, branch, head, local, base, first, count, place):
        def to_peer(j, carry):
            peer = base + first + j
            source = result.at[slot, pl.ds(pl.multiple_of((first + j) * local, local), local)]
            target = out.at[branch, :, columns(head)]

            @pl.when(peer == me)
            def _():
                pltpu.make_async_copy(source, target, back_sems.at[place]).start()

            @pl.when(peer != me)
            def _():
                pltpu.make_async_remote_copy(
                    src_ref=source,
                    dst_ref=target,
                    send_sem=send_sems.at[10 + place],
                    recv_sem=back_sems.at[place],
                    device_id=(group, peer),
                    device_id_type=MESH,
                ).start()

            return carry

        lax.fori_loop(0, count, to_peer, 0)

    def part_kinds(source, slot, target):
        for first in range(0, target.shape[1], HEAD):
            here = slice(first, first + HEAD)
            target[:, here] = jnp.swapaxes(source[slot, here], 0, 1)

    def video_item(slot):
        branch, head = video_place(me, slot)
        settle(video_qkv_in.at[slot], video_sems.at[slot])
        block = video_block * video_local

        def rows(i, inner):
            here = pl.ds(pl.multiple_of(i * block, block), block)
            own, _ = attend(
                video_qkv_in[slot, 0, here], video_qkv_in[slot, 1], video_qkv_in[slot, 2], None
            )
            video_res[slot, here] = own.astype(jnp.bfloat16)
            give_back(
                video_res, slot, own_home, branch, head, video_local, 0, i * video_block,
                video_block, 0,
            )
            return inner

        lax.fori_loop(0, n // video_block, rows, 0)

    def cross_item(slot, carry):
        branch, head = cross_place(me, slot)
        settle(video_q_in.at[slot], cross_sems.at[slot, 0])
        settle(audio_kv_in.at[slot], cross_sems.at[slot, 1])
        part_kinds(audio_kv_in, slot, audio_pair)
        block = video_block * video_local

        def rows(i, inner):
            here = pl.ds(pl.multiple_of(i * block, block), block)
            cross, _ = attend(
                video_q_in[slot, here], audio_pair[0], audio_pair[1], mask(branch)
            )
            cross_res[slot, here] = cross.astype(jnp.bfloat16)
            give_back(
                cross_res, slot, cross_home, branch, head, video_local, half_first,
                i * video_block, video_block, 2,
            )
            return inner

        lax.fori_loop(0, near // video_block, rows, 0)
        return carry

    partner = (3 - me // quarter) * quarter + lax.rem(me, quarter)
    half_audio = near * audio_local
    chunks = n * audio_local // HEAD
    half_chunks = chunks // 2

    def half_mask(branch):
        positions = lax.broadcasted_iota(jnp.int32, (1, half_audio), 1) + my_half * half_audio
        return jnp.where(positions < audio_valid[branch], 0.0, -1e30)

    def to_partner(source, target, place, slot):
        pltpu.make_async_remote_copy(
            src_ref=source.at[slot],
            dst_ref=target.at[slot],
            send_sem=send_sems.at[13 + place],
            recv_sem=pair_sems.at[place, slot],
            device_id=(group, partner),
            device_id_type=MESH,
        ).start()

    def audio_item(slot):
        branch, head = audio_place(me, slot)
        settle(both_q_in.at[slot], both_sems.at[slot])
        settle(own_kv_in.at[slot], kv_sems.at[slot, 0])
        settle(video_kv_in.at[slot], kv_sems.at[slot, 1])
        part_kinds(video_kv_in, slot, video_pair)
        block = audio_block * audio_local
        per_block = block // HEAD

        def rows(i, inner):
            here = pl.ds(pl.multiple_of(i * block, block), block)
            for kind, (keys, bias) in enumerate(
                ((own_kv_in.at[slot], half_mask(branch)), (video_pair, None))
            ):
                part, level = attend(both_q_in[slot, kind, here], keys[0], keys[1], bias)
                part_res[slot, kind, here] = part
                for c in range(per_block):
                    column = jnp.broadcast_to(level[c * HEAD : (c + 1) * HEAD], (HEAD, HEAD))
                    level_res[slot, kind * chunks + i * per_block + c] = jnp.transpose(column)[0:1]
            return inner

        lax.fori_loop(0, n // audio_block, rows, 0)
        to_partner(level_res, level_in, 0, slot)

    def weighted(slot, chunk, gate):
        here = pl.ds(pl.multiple_of(chunk * HEAD, HEAD), HEAD)
        terms = []
        for kind in range(2):
            gap = level_in[slot, kind * chunks + chunk] - level_res[slot, kind * chunks + chunk]
            weight = jnp.transpose(jnp.broadcast_to(1.0 / (1.0 + jnp.exp(gap)), (HEAD, HEAD)))
            terms.append(weight * part_res[slot, kind, here])
        return terms[0] + gate * terms[1]

    def audio_share(slot):
        branch, head = audio_place(me, slot)
        settle(level_in.at[slot], pair_sems.at[0, slot])
        gate = gate_of(branch_prompt, audio_gate, branch, columns(head))
        for c in range(half_chunks):
            share_res[slot, c * HEAD : (c + 1) * HEAD] = weighted(
                slot, (1 - my_half) * half_chunks + c, gate
            ).astype(jnp.bfloat16)
        to_partner(share_res, share_in, 1, slot)

    def audio_final(slot):
        branch, head = audio_place(me, slot)
        settle(share_in.at[slot], pair_sems.at[1, slot])
        gate = gate_of(branch_prompt, audio_gate, branch, columns(head))
        for c in range(half_chunks):
            here = slice(c * HEAD, (c + 1) * HEAD)
            final_res[slot, here] = (
                weighted(slot, my_half * half_chunks + c, gate)
                + share_in[slot, here].astype(jnp.float32)
            ).astype(jnp.bfloat16)
        give_back(
            final_res, slot, audio_out, branch, head, audio_local, half_first, 0, near, 1
        )

    my_video = video_outer + inner * (video_inner - video_outer)
    my_audio = audio_outer + inner * (audio_inner - audio_outer)

    def audio_steps(step, work):
        def one(slot, carry):
            work(slot)
            return carry

        first, last = (audio_before(jnp.maximum(edge, 0)) for edge in (step, step + 1))
        lax.fori_loop(jnp.minimum(first, my_audio), jnp.minimum(last, my_audio), one, 0)

    def work_step(step, carry):
        @pl.when(step + AHEAD < steps)
        def _():
            send_step(step + AHEAD, 0)

        audio_steps(step, audio_item)

        @pl.when(step < my_video)
        def _():
            video_item(step)

        audio_steps(step - 1, audio_share)

        lax.fori_loop(cross_before(step), cross_before(step + 1), cross_item, 0)

        audio_steps(step - 2, audio_final)

        return carry

    lax.fori_loop(0, steps, work_step, 0)

    settle(own_home, back_sems.at[0])
    settle(cross_home, back_sems.at[2])
    settle(audio_out, back_sems.at[1])

    far_half = pl.ds(0, (near - 1) * video_local)
    far_video = pl.ds(0, (n - 1) * video_local)

    def few(count, local):
        return pl.ds(0, count * local)

    settle(video_qkv_in.at[0:video_outer, :, far_video], send_sems.at[0])
    settle(video_q_in.at[:, far_half], send_sems.at[2])
    settle(audio_kv_in.at[:, few(n - 1, audio_local)], send_sems.at[3])
    settle(both_q_in.at[0:audio_inner, :, few(n - 1, audio_local)], send_sems.at[4])
    settle(own_kv_in.at[0:audio_inner, :, few(near - 1, audio_local)], send_sems.at[6])
    settle(video_kv_in.at[0:audio_inner, far_half], send_sems.at[7])
    settle(cross_res.at[:, far_half], send_sems.at[12])

    for here in range(2):

        @pl.when(inner == here)
        def _():
            away = 1 - here
            more_video = pl.ds(video_outer, video_inner - video_outer)
            more_audio = pl.ds(audio_inner, audio_outer - audio_inner)
            videos = pl.ds(0, (video_outer, video_inner)[here])
            audios = pl.ds(0, (audio_outer, audio_inner)[here])
            settle(video_qkv_in.at[more_video, :, few(2 * quarter - here, video_local)], send_sems.at[1])
            settle(both_q_in.at[more_audio, :, few(2 * quarter - away, audio_local)], send_sems.at[5])
            settle(own_kv_in.at[more_audio, :, few(quarter - away, audio_local)], send_sems.at[8])
            settle(video_kv_in.at[more_audio, few(quarter - away, video_local)], send_sems.at[9])
            settle(video_res.at[videos, far_video], send_sems.at[10])
            settle(final_res.at[audios, few(near - 1, audio_local)], send_sems.at[11])
            settle(level_res.at[audios], send_sems.at[13])
            settle(share_res.at[audios], send_sems.at[14])


def kinds_first(source):
    return jnp.transpose(source, (0, 2, 1, 3))


def shares(total):
    return total // 4, total - total // 4


def on_device(
    n,
    video_qkv,
    video_cross_q,
    audio_kv_v,
    audio_qkv,
    audio_cross_q,
    video_kv_a,
    audio_valid,
    branch_prompt,
    video_gate,
    audio_gate,
):
    branches, video_local = video_cross_q.shape[:2]
    audio_local = audio_cross_q.shape[1]
    video_all, audio_all = video_local * n, audio_local * n
    near, quarter = n // 2, n // 4
    video_outer, video_inner = shares(branches * HV // near)
    cross_count = branches * HV // near
    audio_inner, audio_outer = shares(branches * HA // quarter)
    hbm = pl.BlockSpec(memory_space=pltpu.HBM)
    vmem = pl.BlockSpec(memory_space=pltpu.VMEM)
    half = jnp.bfloat16
    homes = pl.pallas_call(
        functools.partial(
            block_kernel,
            n,
            video_outer,
            video_inner,
            cross_count,
            audio_outer,
            audio_inner,
            min(2, near),
            min(4, n),
        ),
        out_shape=(
            jax.ShapeDtypeStruct(video_cross_q.shape, half),
            jax.ShapeDtypeStruct(video_cross_q.shape, half),
            jax.ShapeDtypeStruct(audio_cross_q.shape, half),
            jax.ShapeDtypeStruct((branches, video_gate.shape[1]), jnp.float32),
        ),
        in_specs=[hbm] * 10,
        out_specs=(vmem,) * 4,
        scratch_shapes=[
            pltpu.VMEM(video_gate.shape, jnp.float32),
            pltpu.VMEM(audio_gate.shape, jnp.float32),
            pltpu.SMEM(audio_valid.shape, jnp.int32),
            pltpu.SMEM(branch_prompt.shape, jnp.int32),
            pltpu.VMEM((video_inner, 3, video_all, HEAD), half),
            pltpu.VMEM((cross_count, near * video_local, HEAD), half),
            pltpu.VMEM((cross_count, audio_all, 2, HEAD), half),
            pltpu.VMEM((audio_outer, 2, audio_all, HEAD), half),
            pltpu.VMEM((audio_outer, 2, near * audio_local, HEAD), half),
            pltpu.VMEM((audio_outer, near * video_local, 2, HEAD), half),
            pltpu.VMEM((2, audio_all, HEAD), half),
            pltpu.VMEM((2, near * video_local, HEAD), half),
            pltpu.VMEM((video_inner, video_all, HEAD), half),
            pltpu.VMEM((cross_count, near * video_local, HEAD), half),
            pltpu.VMEM((audio_outer, 2, audio_all, HEAD), jnp.float32),
            pltpu.VMEM((audio_outer, 2 * audio_all // HEAD, 1, HEAD), jnp.float32),
            pltpu.VMEM((audio_outer, 2 * audio_all // HEAD, 1, HEAD), jnp.float32),
            pltpu.VMEM((audio_outer, near * audio_local, HEAD), half),
            pltpu.VMEM((audio_outer, near * audio_local, HEAD), half),
            pltpu.VMEM((audio_outer, near * audio_local, HEAD), half),
            pltpu.SemaphoreType.DMA((video_inner,)),
            pltpu.SemaphoreType.DMA((cross_count, 2)),
            pltpu.SemaphoreType.DMA((audio_outer,)),
            pltpu.SemaphoreType.DMA((audio_outer, 2)),
            pltpu.SemaphoreType.DMA((2, audio_outer)),
            pltpu.SemaphoreType.DMA((15,)),
            pltpu.SemaphoreType.DMA((3,)),
            pltpu.SemaphoreType.DMA((4,)),
        ],
        compiler_params=pltpu.CompilerParams(
            collective_id=0, has_side_effects=True, vmem_limit_bytes=48 * 2**20
        ),
    )(
        *(
            pltpu.with_memory_space_constraint(source, pltpu.HBM)
            for source in (
                kinds_first(video_qkv),
                video_cross_q,
                audio_kv_v,
                kinds_first(audio_qkv),
                audio_cross_q,
                video_kv_a,
                video_gate,
                audio_gate,
                audio_valid,
                branch_prompt,
            )
        )
    )
    return tuple(
        pl.pallas_call(
            join_kernel,
            out_shape=(
                jax.ShapeDtypeStruct(video_cross_q.shape, half),
                jax.ShapeDtypeStruct(audio_cross_q.shape, half),
            ),
            in_specs=[vmem] * 4,
            out_specs=(hbm, hbm),
            scratch_shapes=[
                pltpu.VMEM(video_cross_q.shape, half),
                pltpu.SemaphoreType.DMA((branches * video_cross_q.shape[2] // JOIN + 1,)),
            ],
            compiler_params=pltpu.CompilerParams(vmem_limit_bytes=4 * 2**20),
        )(*homes)
    )


def solution(mesh):
    placed = (
        P("groups", "seq", None, None),
        P("groups", "seq", None),
        P("groups", "seq", None, None),
        P("groups", "seq", None, None),
        P("groups", "seq", None),
        P("groups", "seq", None, None),
        P("groups"),
        P("groups"),
        P(),
        P(),
    )
    return jax.shard_map(
        functools.partial(on_device, mesh.shape["seq"]),
        mesh=mesh,
        in_specs=placed,
        out_specs=(P("groups", "seq", None), P("groups", "seq", None)),
        check_vma=False,
    )
```

```python
import functools

import jax
import jax.numpy as jnp
from jax import lax
from jax.experimental import pallas as pl
from jax.experimental.pallas import tpu as pltpu
from jax.sharding import PartitionSpec as P

HV = 32
HA = 16
HEAD = 128
PROMPTS = 4
MESH = pl.DeviceIdType.MESH
AHEAD = 2
JOIN = 1024


def attend(queries, key_rows, value_rows, bias):
    scores = lax.dot_general(
        queries, key_rows, (((1,), (1,)), ((), ())), preferred_element_type=jnp.float32
    ) * (HEAD**-0.5)
    if bias is not None:
        scores = scores + bias
    row_max = jnp.max(scores, axis=1, keepdims=True)
    weights = jnp.exp(scores - row_max)
    total = jnp.sum(weights, axis=1, keepdims=True)
    result = jnp.dot(
        weights.astype(jnp.bfloat16), value_rows, preferred_element_type=jnp.float32
    )
    return result / total, row_max + jnp.log(total)


def gate_of(branch_prompt, gates, branch, here):
    return sum(
        (branch_prompt[branch] == p).astype(jnp.int32).astype(jnp.float32)
        * gates[p : p + 1, here]
        for p in range(PROMPTS)
    )


def join_kernel(
    own_home, cross_home, audio_home, video_gates, video_out, audio_out, joined, sems
):
    width = JOIN
    branches, parts = own_home.shape[0], own_home.shape[2] // width
    audio = pltpu.make_async_copy(audio_home, audio_out, sems.at[branches * parts])
    audio.start()
    for branch in range(branches):
        for i in range(parts):
            here = slice(i * width, (i + 1) * width)
            joined[branch, :, here] = (
                own_home[branch, :, here].astype(jnp.float32)
                + video_gates[branch : branch + 1, here]
                * cross_home[branch, :, here].astype(jnp.float32)
            ).astype(jnp.bfloat16)
            pltpu.make_async_copy(
                joined.at[branch, :, here], video_out.at[branch, :, here], sems.at[branch * parts + i]
            ).start()
    for branch in range(branches):
        for i in range(parts):
            here = slice(i * width, (i + 1) * width)
            pltpu.make_async_copy(
                joined.at[branch, :, here], video_out.at[branch, :, here], sems.at[branch * parts + i]
            ).wait()
    audio.wait()


def block_kernel(
    n,
    video_outer,
    video_inner,
    cross_count,
    audio_outer,
    audio_inner,
    video_block,
    audio_block,
    video_qkv,
    video_q,
    audio_kv,
    audio_qkv,
    audio_q,
    video_kv,
    video_gate_far,
    audio_gate_far,
    audio_valid_far,
    branch_prompt_far,
    own_home,
    cross_home,
    audio_out,
    video_gates,
    video_gate,
    audio_gate,
    audio_valid,
    branch_prompt,
    video_qkv_in,
    video_q_in,
    audio_kv_in,
    both_q_in,
    own_kv_in,
    video_kv_in,
    audio_pair,
    video_pair,
    video_res,
    cross_res,
    part_res,
    level_res,
    level_in,
    share_res,
    share_in,
    final_res,
    video_sems,
    cross_sems,
    both_sems,
    kv_sems,
    pair_sems,
    send_sems,
    back_sems,
    small_sems,
):
    me = lax.axis_index("seq")
    group = lax.axis_index("groups")
    video_local = own_home.shape[1]
    audio_local = audio_out.shape[1]

    barrier = pltpu.get_barrier_semaphore()

    def greet(k, carry):
        peer = lax.rem(me + k, n)
        pl.semaphore_signal(barrier, inc=1, device_id=(group, peer), device_id_type=MESH)
        return carry

    lax.fori_loop(1, n, greet, 0)
    small = [
        pltpu.make_async_copy(source, target, small_sems.at[i])
        for i, (source, target) in enumerate(
            (
                (video_gate_far, video_gate),
                (audio_gate_far, audio_gate),
                (audio_valid_far, audio_valid),
                (branch_prompt_far, branch_prompt),
            )
        )
    ]
    for copy in small:
        copy.start()
    pl.semaphore_wait(barrier, n - 1)

    video_rows = pl.ds(pl.multiple_of(me * video_local, video_local), video_local)
    audio_rows = pl.ds(pl.multiple_of(me * audio_local, audio_local), audio_local)

    near, quarter = n // 2, n // 4
    my_half = me // near
    half_first = my_half * near
    place_in_half = me - half_first
    half_rows = pl.ds(pl.multiple_of(place_in_half * video_local, video_local), video_local)
    half_audio_rows = pl.ds(pl.multiple_of(place_in_half * audio_local, audio_local), audio_local)

    def is_inner(device):
        q = device // quarter
        return (q * (3 - q)) // 2

    inner = is_inner(me)
    outer_in_half = my_half * 3 * quarter

    def columns(head):
        return pl.ds(pl.multiple_of(head * HEAD, HEAD), HEAD)

    def video_place(device, slot):
        here = is_inner(device)
        high = device // near
        outside = (device - high * 2 * quarter) * video_outer + slot
        inside = 2 * quarter * video_outer + (device - quarter) * video_inner + slot
        item = outside + here * (inside - outside)
        return item // HV, lax.rem(item, HV)

    def cross_place(device, slot):
        item = lax.rem(device, near) * cross_count + slot
        return item // HV, lax.rem(item, HV)

    def audio_place(device, slot):
        here = is_inner(device)
        r = lax.rem(device, quarter)
        outside = r * audio_outer + slot
        inside = quarter * audio_outer + r * audio_inner + slot
        item = outside + here * (inside - outside)
        return item // HA, lax.rem(item, HA)

    def video_parts(peer, slot):
        branch, head = video_place(peer, slot)
        return (
            (
                video_qkv.at[branch, :, :, columns(head)],
                video_qkv_in.at[slot, :, video_rows],
                video_sems.at[slot],
            ),
        )

    def cross_q_parts(peer, slot):
        branch, head = cross_place(peer, slot)
        return (
            (
                video_q.at[branch, :, columns(head)],
                video_q_in.at[slot, half_rows],
                cross_sems.at[slot, 0],
            ),
        )

    def cross_kv_parts(peer, slot):
        branch, head = cross_place(peer, slot)
        return (
            (
                audio_kv.at[branch, :, :, columns(head)],
                audio_kv_in.at[slot, audio_rows],
                cross_sems.at[slot, 1],
            ),
        )

    def both_q_parts(peer, slot):
        branch, head = audio_place(peer, slot)
        return (
            (
                audio_qkv.at[branch, 0, :, columns(head)],
                both_q_in.at[slot, 0, audio_rows],
                both_sems.at[slot],
            ),
            (
                audio_q.at[branch, :, columns(head)],
                both_q_in.at[slot, 1, audio_rows],
                both_sems.at[slot],
            ),
        )

    def own_kv_parts(peer, slot):
        branch, head = audio_place(peer, slot)
        return (
            (
                audio_qkv.at[branch, 1:3, :, columns(head)],
                own_kv_in.at[slot, :, half_audio_rows],
                kv_sems.at[slot, 0],
            ),
        )

    def video_kv_parts(peer, slot):
        branch, head = audio_place(peer, slot)
        return (
            (
                video_kv.at[branch, :, :, columns(head)],
                video_kv_in.at[slot, half_rows],
                kv_sems.at[slot, 1],
            ),
        )

    def send(parts, slot, send_sem, first, span):
        place = lax.rem(me - first + n, n)
        member = 1 - jnp.minimum(place // span, 1)

        def to_peer(k, carry):
            step = k // 2 + lax.rem(k, 2) * (span // 2)
            peer = lax.rem(first + lax.rem(place + step, span), n)
            for source, target, sem in parts(peer, slot):
                pltpu.make_async_remote_copy(
                    src_ref=source,
                    dst_ref=target,
                    send_sem=send_sems.at[send_sem],
                    recv_sem=sem,
                    device_id=(group, peer),
                    device_id_type=MESH,
                ).start()
            return carry

        lax.fori_loop(member, span, to_peer, 0)

        @pl.when(member == 1)
        def _():
            for source, target, sem in parts(me, slot):
                pltpu.make_async_copy(source, target, sem).start()

    steps = video_inner + 1

    def cross_before(step):
        return (step * cross_count + steps // 2) // steps

    def audio_before(step):
        return jnp.minimum(step + jnp.minimum(step // 2, 1), audio_outer)

    def send_step(step, carry):
        def send_cross(slot, inner_carry):
            send(cross_kv_parts, slot, 3, 0, n)
            send(cross_q_parts, slot, 2, half_first, near)
            return inner_carry

        lax.fori_loop(cross_before(step), cross_before(step + 1), send_cross, 0)
        @pl.when(step < video_outer)
        def _():
            send(video_parts, step, 0, 0, n)

        @pl.when((step >= video_outer) & (step < video_inner))
        def _():
            send(video_parts, step, 1, quarter, 2 * quarter)

        def send_audio(slot, inner_carry):
            @pl.when(slot < audio_inner)
            def _():
                send(both_q_parts, slot, 4, 0, n)
                send(own_kv_parts, slot, 6, half_first, near)
                send(video_kv_parts, slot, 7, half_first, near)

            @pl.when(slot >= audio_inner)
            def _():
                send(both_q_parts, slot, 5, 3 * quarter, 2 * quarter)
                send(own_kv_parts, slot, 8, outer_in_half, quarter)
                send(video_kv_parts, slot, 9, outer_in_half, quarter)

            return inner_carry

        lax.fori_loop(audio_before(step), audio_before(step + 1), send_audio, 0)


        return carry

    lax.fori_loop(0, min(AHEAD, steps), send_step, 0)
    for copy in small:
        copy.wait()
    for branch in range(own_home.shape[0]):
        for first in range(0, own_home.shape[2], JOIN):
            here = slice(first, first + JOIN)
            video_gates[branch : branch + 1, here] = gate_of(branch_prompt, video_gate, branch, here)

    def mask(branch):
        positions = lax.broadcasted_iota(jnp.int32, (1, audio_kv_in.shape[1]), 1)
        return jnp.where(positions < audio_valid[branch], 0.0, -jnp.inf)

    def settle(ref, sem):
        pltpu.make_async_copy(ref, ref, sem).wait()

    def give_back(result, slot, out, branch, head, local, base, first, count, place):
        def to_peer(j, carry):
            peer = base + first + j
            source = result.at[slot, pl.ds(pl.multiple_of((first + j) * local, local), local)]
            target = out.at[branch, :, columns(head)]

            @pl.when(peer == me)
            def _():
                pltpu.make_async_copy(source, target, back_sems.at[place]).start()

            @pl.when(peer != me)
            def _():
                pltpu.make_async_remote_copy(
                    src_ref=source,
                    dst_ref=target,
                    send_sem=send_sems.at[10 + place],
                    recv_sem=back_sems.at[place],
                    device_id=(group, peer),
                    device_id_type=MESH,
                ).start()

            return carry

        lax.fori_loop(0, count, to_peer, 0)

    def part_kinds(source, slot, target):
        for first in range(0, target.shape[1], HEAD):
            here = slice(first, first + HEAD)
            target[:, here] = jnp.swapaxes(source[slot, here], 0, 1)

    def video_item(slot):
        branch, head = video_place(me, slot)
        settle(video_qkv_in.at[slot], video_sems.at[slot])
        block = video_block * video_local

        def rows(i, inner):
            here = pl.ds(pl.multiple_of(i * block, block), block)
            own, _ = attend(
                video_qkv_in[slot, 0, here], video_qkv_in[slot, 1], video_qkv_in[slot, 2], None
            )
            video_res[slot, here] = own.astype(jnp.bfloat16)
            give_back(
                video_res, slot, own_home, branch, head, video_local, 0, i * video_block,
                video_block, 0,
            )
            return inner

        lax.fori_loop(0, n // video_block, rows, 0)

    def cross_item(slot, carry):
        branch, head = cross_place(me, slot)
        settle(video_q_in.at[slot], cross_sems.at[slot, 0])
        settle(audio_kv_in.at[slot], cross_sems.at[slot, 1])
        part_kinds(audio_kv_in, slot, audio_pair)
        block = video_block * video_local

        def rows(i, inner):
            here = pl.ds(pl.multiple_of(i * block, block), block)
            cross, _ = attend(
                video_q_in[slot, here], audio_pair[0], audio_pair[1], mask(branch)
            )
            cross_res[slot, here] = cross.astype(jnp.bfloat16)
            give_back(
                cross_res, slot, cross_home, branch, head, video_local, half_first,
                i * video_block, video_block, 2,
            )
            return inner

        lax.fori_loop(0, near // video_block, rows, 0)
        return carry

    partner = (3 - me // quarter) * quarter + lax.rem(me, quarter)
    half_audio = near * audio_local
    chunks = n * audio_local // HEAD
    half_chunks = chunks // 2

    def half_mask(branch):
        positions = lax.broadcasted_iota(jnp.int32, (1, half_audio), 1) + my_half * half_audio
        return jnp.where(positions < audio_valid[branch], 0.0, -1e30)

    def to_partner(source, target, place, slot):
        pltpu.make_async_remote_copy(
            src_ref=source.at[slot],
            dst_ref=target.at[slot],
            send_sem=send_sems.at[13 + place],
            recv_sem=pair_sems.at[place, slot],
            device_id=(group, partner),
            device_id_type=MESH,
        ).start()

    def audio_item(slot):
        branch, head = audio_place(me, slot)
        settle(both_q_in.at[slot], both_sems.at[slot])
        settle(own_kv_in.at[slot], kv_sems.at[slot, 0])
        settle(video_kv_in.at[slot], kv_sems.at[slot, 1])
        part_kinds(video_kv_in, slot, video_pair)
        block = audio_block * audio_local
        per_block = block // HEAD

        def rows(i, inner):
            here = pl.ds(pl.multiple_of(i * block, block), block)
            for kind, (keys, bias) in enumerate(
                ((own_kv_in.at[slot], half_mask(branch)), (video_pair, None))
            ):
                part, level = attend(both_q_in[slot, kind, here], keys[0], keys[1], bias)
                part_res[slot, kind, here] = part
                for c in range(per_block):
                    column = jnp.broadcast_to(level[c * HEAD : (c + 1) * HEAD], (HEAD, HEAD))
                    level_res[slot, kind * chunks + i * per_block + c] = jnp.transpose(column)[0:1]
            return inner

        lax.fori_loop(0, n // audio_block, rows, 0)
        to_partner(level_res, level_in, 0, slot)

    def weighted(slot, chunk, gate):
        here = pl.ds(pl.multiple_of(chunk * HEAD, HEAD), HEAD)
        terms = []
        for kind in range(2):
            gap = level_in[slot, kind * chunks + chunk] - level_res[slot, kind * chunks + chunk]
            weight = jnp.transpose(jnp.broadcast_to(1.0 / (1.0 + jnp.exp(gap)), (HEAD, HEAD)))
            terms.append(weight * part_res[slot, kind, here])
        return terms[0] + gate * terms[1]

    def audio_share(slot):
        branch, head = audio_place(me, slot)
        settle(level_in.at[slot], pair_sems.at[0, slot])
        gate = gate_of(branch_prompt, audio_gate, branch, columns(head))
        for c in range(half_chunks):
            share_res[slot, c * HEAD : (c + 1) * HEAD] = weighted(
                slot, (1 - my_half) * half_chunks + c, gate
            ).astype(jnp.bfloat16)
        to_partner(share_res, share_in, 1, slot)

    def audio_final(slot):
        branch, head = audio_place(me, slot)
        settle(share_in.at[slot], pair_sems.at[1, slot])
        gate = gate_of(branch_prompt, audio_gate, branch, columns(head))
        for c in range(half_chunks):
            here = slice(c * HEAD, (c + 1) * HEAD)
            final_res[slot, here] = (
                weighted(slot, my_half * half_chunks + c, gate)
                + share_in[slot, here].astype(jnp.float32)
            ).astype(jnp.bfloat16)
        give_back(
            final_res, slot, audio_out, branch, head, audio_local, half_first, 0, near, 1
        )

    my_video = video_outer + inner * (video_inner - video_outer)
    my_audio = audio_outer + inner * (audio_inner - audio_outer)

    def audio_steps(step, work):
        def one(slot, carry):
            work(slot)
            return carry

        first, last = (audio_before(jnp.maximum(edge, 0)) for edge in (step, step + 1))
        lax.fori_loop(jnp.minimum(first, my_audio), jnp.minimum(last, my_audio), one, 0)

    def work_step(step, carry):
        audio_steps(step, audio_item)

        @pl.when(step + AHEAD < steps)
        def _():
            send_step(step + AHEAD, 0)

        @pl.when(step < my_video)
        def _():
            video_item(step)

        audio_steps(step - 1, audio_share)

        lax.fori_loop(cross_before(step), cross_before(step + 1), cross_item, 0)

        audio_steps(step - 2, audio_final)

        return carry

    lax.fori_loop(0, steps, work_step, 0)

    settle(own_home, back_sems.at[0])
    settle(cross_home, back_sems.at[2])
    settle(audio_out, back_sems.at[1])

    far_half = pl.ds(0, (near - 1) * video_local)
    far_video = pl.ds(0, (n - 1) * video_local)

    def few(count, local):
        return pl.ds(0, count * local)

    settle(video_qkv_in.at[0:video_outer, :, far_video], send_sems.at[0])
    settle(video_q_in.at[:, far_half], send_sems.at[2])
    settle(audio_kv_in.at[:, few(n - 1, audio_local)], send_sems.at[3])
    settle(both_q_in.at[0:audio_inner, :, few(n - 1, audio_local)], send_sems.at[4])
    settle(own_kv_in.at[0:audio_inner, :, few(near - 1, audio_local)], send_sems.at[6])
    settle(video_kv_in.at[0:audio_inner, far_half], send_sems.at[7])
    settle(cross_res.at[:, far_half], send_sems.at[12])

    for here in range(2):

        @pl.when(inner == here)
        def _():
            away = 1 - here
            more_video = pl.ds(video_outer, video_inner - video_outer)
            more_audio = pl.ds(audio_inner, audio_outer - audio_inner)
            videos = pl.ds(0, (video_outer, video_inner)[here])
            audios = pl.ds(0, (audio_outer, audio_inner)[here])
            settle(video_qkv_in.at[more_video, :, few(2 * quarter - here, video_local)], send_sems.at[1])
            settle(both_q_in.at[more_audio, :, few(2 * quarter - away, audio_local)], send_sems.at[5])
            settle(own_kv_in.at[more_audio, :, few(quarter - away, audio_local)], send_sems.at[8])
            settle(video_kv_in.at[more_audio, few(quarter - away, video_local)], send_sems.at[9])
            settle(video_res.at[videos, far_video], send_sems.at[10])
            settle(final_res.at[audios, few(near - 1, audio_local)], send_sems.at[11])
            settle(level_res.at[audios], send_sems.at[13])
            settle(share_res.at[audios], send_sems.at[14])


def kinds_first(source):
    return jnp.transpose(source, (0, 2, 1, 3))


def shares(total):
    return total // 4, total - total // 4


def on_device(
    n,
    video_qkv,
    video_cross_q,
    audio_kv_v,
    audio_qkv,
    audio_cross_q,
    video_kv_a,
    audio_valid,
    branch_prompt,
    video_gate,
    audio_gate,
):
    branches, video_local = video_cross_q.shape[:2]
    audio_local = audio_cross_q.shape[1]
    video_all, audio_all = video_local * n, audio_local * n
    near, quarter = n // 2, n // 4
    video_outer, video_inner = shares(branches * HV // near)
    cross_count = branches * HV // near
    audio_inner, audio_outer = shares(branches * HA // quarter)
    hbm = pl.BlockSpec(memory_space=pltpu.HBM)
    vmem = pl.BlockSpec(memory_space=pltpu.VMEM)
    half = jnp.bfloat16
    homes = pl.pallas_call(
        functools.partial(
            block_kernel,
            n,
            video_outer,
            video_inner,
            cross_count,
            audio_outer,
            audio_inner,
            min(2, near),
            min(4, n),
        ),
        out_shape=(
            jax.ShapeDtypeStruct(video_cross_q.shape, half),
            jax.ShapeDtypeStruct(video_cross_q.shape, half),
            jax.ShapeDtypeStruct(audio_cross_q.shape, half),
            jax.ShapeDtypeStruct((branches, video_gate.shape[1]), jnp.float32),
        ),
        in_specs=[hbm] * 10,
        out_specs=(vmem,) * 4,
        scratch_shapes=[
            pltpu.VMEM(video_gate.shape, jnp.float32),
            pltpu.VMEM(audio_gate.shape, jnp.float32),
            pltpu.SMEM(audio_valid.shape, jnp.int32),
            pltpu.SMEM(branch_prompt.shape, jnp.int32),
            pltpu.VMEM((video_inner, 3, video_all, HEAD), half),
            pltpu.VMEM((cross_count, near * video_local, HEAD), half),
            pltpu.VMEM((cross_count, audio_all, 2, HEAD), half),
            pltpu.VMEM((audio_outer, 2, audio_all, HEAD), half),
            pltpu.VMEM((audio_outer, 2, near * audio_local, HEAD), half),
            pltpu.VMEM((audio_outer, near * video_local, 2, HEAD), half),
            pltpu.VMEM((2, audio_all, HEAD), half),
            pltpu.VMEM((2, near * video_local, HEAD), half),
            pltpu.VMEM((video_inner, video_all, HEAD), half),
            pltpu.VMEM((cross_count, near * video_local, HEAD), half),
            pltpu.VMEM((audio_outer, 2, audio_all, HEAD), jnp.float32),
            pltpu.VMEM((audio_outer, 2 * audio_all // HEAD, 1, HEAD), jnp.float32),
            pltpu.VMEM((audio_outer, 2 * audio_all // HEAD, 1, HEAD), jnp.float32),
            pltpu.VMEM((audio_outer, near * audio_local, HEAD), half),
            pltpu.VMEM((audio_outer, near * audio_local, HEAD), half),
            pltpu.VMEM((audio_outer, near * audio_local, HEAD), half),
            pltpu.SemaphoreType.DMA((video_inner,)),
            pltpu.SemaphoreType.DMA((cross_count, 2)),
            pltpu.SemaphoreType.DMA((audio_outer,)),
            pltpu.SemaphoreType.DMA((audio_outer, 2)),
            pltpu.SemaphoreType.DMA((2, audio_outer)),
            pltpu.SemaphoreType.DMA((15,)),
            pltpu.SemaphoreType.DMA((3,)),
            pltpu.SemaphoreType.DMA((4,)),
        ],
        compiler_params=pltpu.CompilerParams(
            collective_id=0, has_side_effects=True, vmem_limit_bytes=48 * 2**20
        ),
    )(
        *(
            pltpu.with_memory_space_constraint(source, pltpu.HBM)
            for source in (
                kinds_first(video_qkv),
                video_cross_q,
                audio_kv_v,
                kinds_first(audio_qkv),
                audio_cross_q,
                video_kv_a,
                video_gate,
                audio_gate,
                audio_valid,
                branch_prompt,
            )
        )
    )
    return tuple(
        pl.pallas_call(
            join_kernel,
            out_shape=(
                jax.ShapeDtypeStruct(video_cross_q.shape, half),
                jax.ShapeDtypeStruct(audio_cross_q.shape, half),
            ),
            in_specs=[vmem] * 4,
            out_specs=(hbm, hbm),
            scratch_shapes=[
                pltpu.VMEM(video_cross_q.shape, half),
                pltpu.SemaphoreType.DMA((branches * video_cross_q.shape[2] // JOIN + 1,)),
            ],
            compiler_params=pltpu.CompilerParams(vmem_limit_bytes=4 * 2**20),
        )(*homes)
    )


def solution(mesh):
    placed = (
        P("groups", "seq", None, None),
        P("groups", "seq", None),
        P("groups", "seq", None, None),
        P("groups", "seq", None, None),
        P("groups", "seq", None),
        P("groups", "seq", None, None),
        P("groups"),
        P("groups"),
        P(),
        P(),
    )
    return jax.shard_map(
        functools.partial(on_device, mesh.shape["seq"]),
        mesh=mesh,
        in_specs=placed,
        out_specs=(P("groups", "seq", None), P("groups", "seq", None)),
        check_vma=False,
    )
```
